512 devices in a mesh: gx: 16 (over z, y_hi), gy: 32 (over x, y_lo, core).
Axes of the slice: x: 4, y: 8 (y_hi: 2, y_lo: 4; y = y_hi * 4 + y_lo), z: 8, core: 2. Of those that a mesh axis runs over, the one named last changes fastest.
Arguments:
- start_coeffs: float32 [9, 2048, 8192], P(None, 'gy', 'gx'), may hold values from -6 to 6
- section_coeffs: float32 [9, 2048, 8192], P(None, 'gy', 'gx'), may hold values from -6 to 6
- vel_x: float32 [2048, 8192], P('gy', 'gx'), may hold values from -1 to 1
- vel_y: float32 [2048, 8192], P('gy', 'gx'), may hold values from -1 to 1
Outputs:
- updated: float32 [9, 2048, 8192], P(None, 'gy', 'gx')
- filtered: float32 [9, 2048, 8192], P(None, 'gy', 'gx')
The draws below stay inside these ranges and needn't reach their ends.
All inputs are finite; a program needn't handle non-finite values.
Results may differ from the reference program's by a relative error of at most 0.0001.
Values sent between devices are 32-bit elements; how exact they have to be, the bound alone decides.
No kernel may reach another device: no remote copies, remote signals or barrier semaphores. Data moves between devices by JAX's collectives and lax.ppermute only.
A program may use at most 64 MiB of HBM per device.

```python
import jax
import jax.numpy as jnp
import numpy as np
from jax import lax

MODES = 9
NX = 8192
NY = 2048


def level_of(stream_key, extent, cuts, least, top_value):
    def one(axis_at, shards_of):
        draws = jax.random.uniform(jax.random.fold_in(jax.random.fold_in(stream_key, 6), axis_at), (shards_of,), jnp.float32, least / len(cuts), top_value / len(cuts))
        return jnp.repeat(jnp.exp(draws), extent[axis_at] // shards_of).reshape((-1,) + (1,) * (len(extent) - axis_at - 1))

    factor_of = one(*cuts[0])
    for cut in cuts[1:]:
        factor_of = factor_of * one(*cut)
    return factor_of


def bell_draw(key, extent, spread, most, cuts=(), held_as=jnp.bfloat16):
    values = spread * jax.random.normal(key, extent, jnp.float32)
    if cuts:
        values = values * level_of(key, extent, cuts, -0.22, 0.18)
    return jnp.clip(values, -most, most).astype(held_as)


def setup_inputs(seed: int = 0) -> dict:
    keys = jax.random.split(jax.random.key(seed), 5)
    start_coeffs = bell_draw(keys[0], (MODES, NY, NX), 1.0, 6.0, ((1, 32), (2, 16)), jnp.float32)
    section_coeffs = bell_draw(keys[1], (MODES, NY, NX), 1.0, 6.0, ((1, 32), (2, 16)), jnp.float32)
    vel_x = jnp.clip(jax.random.uniform(keys[2], (NY, NX), jnp.float32, -1.0, 1.0) * level_of(keys[2], (NY, NX), ((0, 32), (1, 16)), -0.4, 0.0), -1.0, 1.0)
    vel_y = jnp.clip(jax.random.uniform(keys[3], (NY, NX), jnp.float32, -1.0, 1.0) * level_of(keys[3], (NY, NX), ((0, 32), (1, 16)), -0.4, 0.0), -1.0, 1.0)
    return {"start_coeffs": start_coeffs, "section_coeffs": section_coeffs, "vel_x": vel_x, "vel_y": vel_y}


STEP_SIZE = 0.3
GAUSS_NODES = (-0.9324695142031521, -0.6612093864662645, -0.2386191860831969, 0.2386191860831969, 0.6612093864662645, 0.9324695142031521)
GAUSS_WEIGHTS = (0.1713244923791704, 0.3607615730481386, 0.4679139345726910, 0.4679139345726910, 0.3607615730481386, 0.1713244923791704)


def legendre_rows(points):
    return np.stack([points * 0.0 + 1.0, points, 1.5 * points * points - 0.5])


def bspline(points):
    magnitude = np.abs(points)
    return np.where(magnitude <= 0.5, 0.75 - magnitude * magnitude, np.where(magnitude <= 1.5, 0.5 * (1.5 - magnitude) ** 2, 0.0))


def kernel_value(points):
    return 1.25 * bspline(points) - 0.125 * (bspline(points + 1.0) + bspline(points - 1.0))


def siac_table():
    nodes = np.array(GAUSS_NODES)
    weights = np.array(GAUSS_WEIGHTS)
    kernel_table = np.zeros((5, 3, 3))
    for slot_index in range(5):
        offset = slot_index - 2
        for low_end, high_end in ((-1.0, 0.0), (0.0, 1.0)):
            for node_value, node_weight in zip(GAUSS_NODES, GAUSS_WEIGHTS):
                xi_value = 0.5 * (low_end + high_end) + 0.5 * (high_end - low_end) * node_value
                outer_weight = 0.5 * (high_end - low_end) * node_weight
                breaks = [-1.0, 1.0]
                for spline_knot in (-2.5, -1.5, -0.5, 0.5, 1.5, 2.5):
                    crossing = xi_value - 2.0 * offset - 2.0 * spline_knot
                    if -1.0 < crossing < 1.0:
                        breaks.append(crossing)
                breaks = sorted(breaks)
                for piece_lo, piece_hi in zip(breaks[:-1], breaks[1:]):
                    eta_points = 0.5 * (piece_lo + piece_hi) + 0.5 * (piece_hi - piece_lo) * nodes
                    eta_weights = 0.5 * (piece_hi - piece_lo) * weights
                    samples = kernel_value(0.5 * xi_value - 0.5 * eta_points - offset) * eta_weights * 0.5
                    kernel_table[slot_index] += outer_weight * np.outer(legendre_rows(np.array(xi_value)), legendre_rows(eta_points) @ samples)
    return kernel_table * (np.arange(3)[None, :, None] + 0.5)


def x_faces(coeffs):
    east_side = coeffs[0] + coeffs[1] + coeffs[2]
    west_side = coeffs[0] - coeffs[1] + coeffs[2]
    return east_side, west_side


def y_faces(coeffs):
    north_side = coeffs[:, 0] + coeffs[:, 1] + coeffs[:, 2]
    south_side = coeffs[:, 0] - coeffs[:, 1] + coeffs[:, 2]
    return north_side, south_side


def face_flux(inner, outer, speed_in, speed_out):
    speed = 0.5 * (speed_in + speed_out)
    return speed * (0.5 * (inner + outer)) - (0.5 * jnp.abs(speed)) * (outer - inner)


def tendency(coeffs, vel_x, vel_y, west, east, south, north):
    parity = (1.0, -1.0, 1.0)
    terms = []
    for deg_x in range(3):
        for deg_y in range(3):
            along_x = -(east[deg_y] - parity[deg_x] * west[deg_y])
            if deg_x > 0:
                along_x = 2.0 * vel_x * coeffs[deg_x - 1, deg_y] + along_x
            along_y = -(north[deg_x] - parity[deg_y] * south[deg_x])
            if deg_y > 0:
                along_y = 2.0 * vel_y * coeffs[deg_x, deg_y - 1] + along_y
            terms.append((deg_x + 0.5) * along_x + (deg_y + 0.5) * along_y)
    return jnp.stack(terms)


def advance(start_coeffs, section_coeffs, rate):
    return start_coeffs / 3.0 + (2.0 / 3.0) * (section_coeffs + STEP_SIZE * rate)


def reference(start_coeffs, section_coeffs, vel_x, vel_y):
    coeffs = section_coeffs.reshape(3, 3, NY, NX)
    east_x, west_x = x_faces(coeffs)
    east = face_flux(east_x, jnp.roll(west_x, -1, axis=-1), vel_x, jnp.roll(vel_x, -1, axis=-1))
    west = jnp.roll(east, 1, axis=-1)
    north_y, south_y = y_faces(coeffs)
    north = face_flux(north_y, jnp.roll(south_y, -1, axis=-2), vel_y, jnp.roll(vel_y, -1, axis=-2))
    south = jnp.roll(north, 1, axis=-2)
    rate = tendency(coeffs, vel_x, vel_y, west, east, south, north)
    updated = advance(start_coeffs, section_coeffs, rate)
    kernel_table = jnp.asarray(siac_table(), dtype=jnp.float32)
    grid = updated.reshape(3, 3, NY, NX)
    swept = None
    for slot in range(5):
        piece = jnp.roll(grid, 2 - slot, axis=-1)
        term = jnp.einsum('ac,cbyx->abyx', kernel_table[slot], piece, precision=lax.Precision.HIGHEST)
        swept = term if swept is None else swept + term
    filtered = None
    for slot in range(5):
        piece = jnp.roll(swept, 2 - slot, axis=-2)
        term = jnp.einsum('bd,adyx->abyx', kernel_table[slot], piece, precision=lax.Precision.HIGHEST)
        filtered = term if filtered is None else filtered + term
    return updated, filtered.reshape(9, NY, NX)
```

```python
import functools

import jax
import jax.numpy as jnp
import numpy as np
from jax import lax
from jax.experimental import pallas as pl
from jax.experimental.pallas import tpu as pltpu
from jax.sharding import PartitionSpec as P


HALF = np.arange(3) + 0.5
PARITY = np.array([1.0, -1.0, 1.0])
GAUSS_NODES = (
    -0.932469514203152,
    -0.6612093864662645,
    -0.2386191860831969,
    0.2386191860831969,
    0.6612093864662645,
    0.932469514203152,
)
GAUSS_WEIGHTS = (
    0.1713244923791704,
    0.3607615730481386,
    0.467913934572691,
    0.467913934572691,
    0.3607615730481386,
    0.1713244923791704,
)
HIGHEST = lax.Precision.HIGHEST
F32 = jnp.float32


def legendre_rows(points):
    return np.stack([points * 0.0 + 1.0, points, 1.5 * points * points - 0.5])


def bspline(points):
    magnitude = np.abs(points)
    return np.where(
        magnitude <= 0.5,
        0.75 - magnitude * magnitude,
        np.where(magnitude <= 1.5, 0.5 * (1.5 - magnitude) ** 2, 0.0),
    )


def kernel_value(points):
    return 1.25 * bspline(points) - 0.125 * (bspline(points + 1.0) + bspline(points - 1.0))


def siac_table():
    nodes = np.array(GAUSS_NODES)
    weights = np.array(GAUSS_WEIGHTS)
    kernel_table = np.zeros((5, 3, 3))
    for slot_index in range(5):
        offset = slot_index - 2
        for low_end, high_end in ((-1.0, 0.0), (0.0, 1.0)):
            for node_value, node_weight in zip(GAUSS_NODES, GAUSS_WEIGHTS):
                xi_value = 0.5 * (low_end + high_end) + 0.5 * (high_end - low_end) * node_value
                outer_weight = 0.5 * (high_end - low_end) * node_weight
                breaks = [-1.0, 1.0]
                for spline_knot in (-2.5, -1.5, -0.5, 0.5, 1.5, 2.5):
                    crossing = xi_value - 2.0 * offset - 2.0 * spline_knot
                    if -1.0 < crossing < 1.0:
                        breaks.append(crossing)
                breaks = sorted(breaks)
                for piece_lo, piece_hi in zip(breaks[:-1], breaks[1:]):
                    eta_points = 0.5 * (piece_lo + piece_hi) + 0.5 * (piece_hi - piece_lo) * nodes
                    eta_weights = 0.5 * (piece_hi - piece_lo) * weights
                    samples = (
                        kernel_value(0.5 * xi_value - 0.5 * eta_points - offset) * eta_weights * 0.5
                    )
                    kernel_table[slot_index] += outer_weight * np.outer(
                        legendre_rows(np.array(xi_value)), legendre_rows(eta_points) @ samples
                    )
    table = kernel_table * (np.arange(3)[None, :, None] + 0.5)
    return table.astype(np.float32).astype(np.float64)


TABLE = siac_table()


def tap(k):
    return TABLE[k + 2] if abs(k) <= 2 else np.zeros((3, 3))


def column_matrices():
    out = np.zeros((2, 128, 256))
    for group in range(4):
        base = 32 * group
        for b in range(3):
            for a in range(3):
                m_out = 3 * a + b
                for i in range(3):
                    col = base + 3 * m_out + i
                    for side, (first, near, far) in enumerate(((-2, -1, 0), (3, 2, 3))):
                        for c in range(3):
                            for j in range(2):
                                out[side, base + 2 * (3 * c + b) + j, col] += tap(first + j - i)[a, c]
                        flux = tap(near - i)[a] @ -HALF + tap(far - i)[a] @ (HALF * PARITY)
                        out[side, base + 18 + b, col] += flux
                out[0, base + 18 + b, 128 + base + m_out] += HALF[a] * PARITY[a]
                out[1, base + 18 + b, 128 + base + m_out] += -HALF[a]
    return out.astype(np.float32)


def row_matrices():
    out = np.zeros((2, 144, 64))
    for a in range(3):
        for b in range(3):
            m_out = 3 * a + b
            for i in range(3):
                for side, (first, near, far, row) in enumerate(((-2, -1, 0, i), (3, 2, 3, 5 + i))):
                    for d in range(3):
                        for j in range(2):
                            out[side, 8 * m_out + row, 9 * j + 3 * a + d] += tap(first + j - i)[b, d]
                    weight = tap(near - i)[b] @ -HALF + tap(far - i)[b] @ (HALF * PARITY)
                    for k in range(-2, 3):
                        for c in range(3):
                            out[side, 8 * m_out + row, 24 + 8 * (k + 2) + 2 + c] += tap(k)[a, c] * weight
            out[0, 72 + 8 * m_out, 24 + 16 + 2 + a] = HALF[b] * PARITY[b]
            out[1, 72 + 8 * m_out + 7, 24 + 16 + 2 + a] = -HALF[b]
    return out.astype(np.float32)


def upwind(speed, inner, outer):
    return jnp.maximum(speed, 0.0) * inner + jnp.minimum(speed, 0.0) * outer


def tile_iota(shape, dim):
    return lax.broadcasted_iota(jnp.int32, shape, dim)


def rows_of(r, count=8, first=0):
    return pl.ds(pl.multiple_of(count * r + first, 8), count)


def turned(value, shift, axis):
    shift %= value.shape[axis]
    return pltpu.roll(value, shift, axis) if shift else value


def update_terms(u, begin, speed_x, speed_y, faces_x, jumps_y):
    sixth_x, sixth_y = 0.6 * speed_x, 0.6 * speed_y
    for b in range(3):
        jump, total = faces_x(b)
        for a in range(3):
            m = 3 * a + b
            value = begin(m) * (1.0 / 3.0) + u[m] * (2.0 / 3.0)
            if a == 0:
                value = value - 0.5 * jump
            elif a == 1:
                value = value + (sixth_x * u[b] - 1.5 * total)
            else:
                value = value + (speed_x * u[3 + b] - 2.5 * jump)
            if b == 0:
                value = value - 0.5 * jumps_y(a, 0)
            elif b == 1:
                value = value + (sixth_y * u[3 * a] - 1.5 * jumps_y(a, 1))
            else:
                value = value + (speed_y * u[3 * a + 1] - 2.5 * jumps_y(a, 0))
            yield m, value


def pack_kernel(width, height, start, sect, vel_x, vel_y, west, east, send_odd, send_even, s, u, vx, vy, jumps, packed, sems):
    copies = []
    for side in range(2):
        cols = pl.ds(side * (width - 128), 128)
        copies.append([
            pltpu.make_async_copy(source.at[..., cols], target.at[side], sems.at[4 * side + n])
            for n, (source, target) in enumerate(((sect, u), (vel_y, vy), (vel_x, vx), (start, s)))
        ])
        for copy in copies[side]:
            copy.start()
    row = tile_iota((height, 128), 0)
    span = 16
    lane = tile_iota((span, 128), 1)
    for side in range(2):
        extra = 2 * side
        copies[side][0].wait()
        copies[side][1].wait()
        speeds = vy[side]
        speed = jnp.where(row == 0, 0.0, 0.1 * (speeds + pltpu.roll(speeds, 1, 0)))
        high, low = jnp.maximum(speed, 0.0), jnp.minimum(speed, 0.0)
        for a in range(3):
            even, odd = u[side, 3 * a] + u[side, 3 * a + 2], u[side, 3 * a + 1]
            north, south = even + odd, even - odd
            face = high * pltpu.roll(north, 1, 0) + low * south
            above = pltpu.roll(face, height - 1, 0)
            jumps[a] = above - face
            jumps[3 + a] = above + face
            jumps[6 + a] = jnp.where(row < height // 2, south, north)
        copies[side][2].wait()
        copies[side][3].wait()

        def cells(r, carry, side=side, extra=extra):
            rows = rows_of(r, span)
            modes = [u[side, m, rows, :] for m in range(9)]
            speed_x, speed_y = vx[side, rows, :], vy[side, rows, :]
            speed = jnp.where(lane == 0, 0.0, 0.1 * (speed_x + pltpu.roll(speed_x, 1, 1)))
            high, low = jnp.maximum(speed, 0.0), jnp.minimum(speed, 0.0)
            acc = turned(speed_x, 21 + extra // 2, 1)
            acc = jnp.where(lane == 22, turned(speed_x, 22 + extra // 2, 1), acc)
            acc = jnp.where(lane == 23, turned(speed_x, 23 + extra // 2, 1), acc)

            def put(acc, value, at, count):
                if count == 2:
                    return jnp.where((lane == at) | (lane == at + 1), turned(value, at + extra, 1), acc)
                return jnp.where(lane == at, turned(value, at + extra // 2, 1), acc)

            def faces_x(b):
                nonlocal acc
                even, odd = modes[b] + modes[6 + b], modes[3 + b]
                face = high * pltpu.roll(even + odd, 1, 1) + low * (even - odd)
                beyond = pltpu.roll(face, 127, 1)
                acc = put(acc, even + odd if side else even - odd, 18 + b, 1)
                return beyond - face, beyond + face

            terms = update_terms(
                modes,
                lambda m: s[side, m, rows, :],
                speed_x,
                speed_y,
                faces_x,
                lambda a, kind: jumps[3 * kind + a, rows, :],
            )
            for m, value in terms:
                acc = put(acc, value, 2 * m, 2)
            for a in range(3):
                acc = put(acc, jumps[6 + a, rows, :], 24 + 2 * a, 2)
            acc = put(acc, speed_y, 30, 2)
            packed[side, rows, :] = acc
            return carry

        lax.fori_loop(0, height // span, cells, 0)
    odd_column = lax.rem(lax.axis_index("gx"), 2) == 1
    slot = tile_iota((16, 128), 1)
    both = []
    for side in range(2):
        acc = packed[side, 0:16, :]
        for group in range(1, 4):
            moved = pltpu.roll(packed[side, 16 * group : 16 * group + 16, :], 32 * group, 1)
            acc = jnp.where(slot >= 32 * group, moved, acc)
        both.append(acc)
    west[...] = both[0]
    east[...] = both[1]
    send_odd[...] = jnp.where(odd_column, both[1], both[0])
    send_even[...] = jnp.where(odd_column, both[0], both[1])


def interior_kernel(width, height, start, sect, vel_x, vel_y, part, swept, traces, s, u, vx, vy, south, sems):
    chunk = 16
    tiles = height // 8
    shape = (8, width)
    lane = tile_iota(shape, 1)
    sub = tile_iota(shape, 0)
    pad = jnp.zeros((8, 128), F32)
    nothing = jnp.zeros(shape, F32)

    small = [
        pltpu.make_async_copy(vel_y, vy, sems.at[0]),
        pltpu.make_async_copy(vel_x, vx, sems.at[1]),
    ]
    small[0].start()
    copies = []
    for n in range(height // chunk):
        rows = pl.ds(chunk * n, chunk)
        copies.append(pltpu.make_async_copy(sect.at[:, rows, :], u.at[:, rows, :], sems.at[2 + n]))
        copies[n].start()
    small[1].start()
    begin = []
    for n in range(height // chunk):
        rows = pl.ds(chunk * n, chunk)
        begin.append(pltpu.make_async_copy(start.at[:, rows, :], s.at[:, rows, :], sems.at[2 + height // chunk + n]))
        begin[n].start()

    def south_faces(r, carry):
        rows = rows_of(r)
        speeds = vy[rows, :]
        turned_speed = pltpu.roll(speeds, 1, 0)
        speed = 0.1 * (speeds + jnp.where(sub == 0, carry[3], turned_speed))
        speed = jnp.where((sub == 0) & (r == 0), 0.0, speed)
        high, low = jnp.maximum(speed, 0.0), jnp.minimum(speed, 0.0)
        ahead = []
        for a in range(3):
            even, odd = u[3 * a, rows, :] + u[3 * a + 2, rows, :], u[3 * a + 1, rows, :]
            north = pltpu.roll(even + odd, 1, 0)
            south[a, rows, :] = high * jnp.where(sub == 0, carry[a], north) + low * (even - odd)
            ahead.append(north)
        return (*ahead, turned_speed)

    def shifted(field, k):
        if k == 0:
            return field[:, :width]
        return pltpu.roll(field, (-k) % (width + 128), 1)[:, :width]

    def cells(r, carry):
        rows = rows_of(r)
        after = rows_of(r, first=8)
        modes = [u[m, rows, :] for m in range(9)]
        speed_x, speed_y = vx[rows, :], vy[rows, :]
        speed = jnp.where(lane == 0, 0.0, 0.1 * (speed_x + pltpu.roll(speed_x, 1, 1)))
        high, low = jnp.maximum(speed, 0.0), jnp.minimum(speed, 0.0)
        jump_y, sum_y = [], []
        for a in range(3):
            face = south[a, rows, :]
            above = jnp.where(sub == 7, pltpu.roll(south[a, after, :], 7, 0), pltpu.roll(face, 7, 0))
            jump_y.append(above - face)
            sum_y.append(above + face)

        def faces_x(b):
            even, odd = modes[b] + modes[6 + b], modes[3 + b]
            face = high * pltpu.roll(even + odd, 1, 1) + low * (even - odd)
            beyond = pltpu.roll(face, width - 1, 1)
            return beyond - face, beyond + face

        fields = []
        terms = update_terms(
            modes, lambda m: s[m, rows, :], speed_x, speed_y, faces_x, lambda a, kind: (sum_y if kind else jump_y)[a]
        )
        for m, value in terms:
            part[m, rows, :] = value
            fields.append(jnp.concatenate([value, pad], axis=1))
            if len(fields) == 3:
                for a, out in enumerate(sweep(fields, shifted)):
                    swept[3 * a + m % 3, after, :] = out
                fields = []
        return carry

    small[0].wait()
    carry = (nothing,) * 4
    for n in range(height // chunk):
        copies[n].wait()
        carry = lax.fori_loop(n * chunk // 8, (n + 1) * chunk // 8, south_faces, carry)
    for a in range(3):
        south[a, height : height + 8, :] = nothing
        even = u[3 * a, 0:8, :] + u[3 * a + 2, 0:8, :]
        traces[a : a + 1, :] = (even - u[3 * a + 1, 0:8, :])[0:1]
        even = u[3 * a, height - 8 :, :] + u[3 * a + 2, height - 8 :, :]
        traces[4 + a : 5 + a, :] = (even + u[3 * a + 1, height - 8 :, :])[7:8]
    traces[3:4, :] = vy[0:1, :]
    traces[7:8, :] = vy[height - 1 :, :]
    for m in range(9):
        swept[m, 0:8, :] = nothing
        swept[m, height + 8 : height + 16, :] = nothing
    small[1].wait()
    for copy in begin:
        copy.wait()
    lax.fori_loop(0, tiles, cells, 0)


def sweep(fields, shifted):
    outs = [None, None, None]

    def add(i, term):
        outs[i] = term if outs[i] is None else outs[i] + term

    for c in range(3):
        for a in range(3):
            if TABLE[2, a, c] != 0.0 and (a + c) % 2 == 0:
                add(a, float(TABLE[2, a, c]) * shifted(fields[c], 0))
        for k in (1, 2):
            ahead, behind = shifted(fields[c], k), shifted(fields[c], -k)
            even, odd = ahead + behind, ahead - behind
            for a in range(3):
                add(a, float(TABLE[2 + k, a, c]) * (even if (a + c) % 2 == 0 else odd))
    return outs


def edge_kernel(width, got_odd, got_even, west, east, low_rows, high_rows, traces, matrices, send_even, send_odd, fixes, buffer):
    odd_column = lax.rem(lax.axis_index("gx"), 2) == 1
    from_west = jnp.where(odd_column, got_even[...], got_odd[...])
    from_east = jnp.where(odd_column, got_odd[...], got_even[...])
    lane16 = tile_iota((16, 128), 1)
    place = jnp.bitwise_and(lane16, 31)
    is_face = (place >= 18) & (place < 21)

    def speed_of(one, two):
        return 0.1 * (pltpu.roll(one, 125, 1) + pltpu.roll(two, 125, 1))

    own_w, own_e = west[...], east[...]
    face_w = upwind(speed_of(from_west, own_w), from_west, own_w)
    face_e = upwind(speed_of(from_east, own_e), own_e, from_east)
    fix_w = jnp.dot(jnp.where(is_face, face_w, from_west), matrices[0], precision=HIGHEST, preferred_element_type=F32)
    fix_e = jnp.dot(jnp.where(is_face, face_e, from_east), matrices[1], precision=HIGHEST, preferred_element_type=F32)
    fixes[0] = fix_w[:, :128]
    fixes[1] = fix_e[:, :128]
    fixes[2] = fix_w[:, 128:]
    fixes[3] = fix_e[:, 128:]

    lane = tile_iota((8, 128), 1)
    buffer[...] = jnp.zeros_like(buffer)
    for side, tile in enumerate((low_rows, high_rows)):
        half, turn = (0, 0) if side == 0 else (1, 32)
        first = 0 if side == 0 else 6
        near_w = fix_w[8 * half : 8 * half + 8, :128]
        near_e = fix_e[8 * half : 8 * half + 8, :128]
        for m in range(9):
            turn_w, turn_e = (turn - 3 * m) % 128, (turn + 125 - 3 * m) % 128
            add_w = jnp.where(lane < 3, pltpu.roll(near_w, turn_w, 1) if turn_w else near_w, 0.0)
            add_e = jnp.where(lane >= 125, pltpu.roll(near_e, turn_e, 1) if turn_e else near_e, 0.0)
            left = tile[m, :, :128] + add_w
            right = tile[m, :, width - 128 :] + add_e
            middle = tile[m, :, 128 : width - 128]
            for j in range(2):
                row = slice(9 * j + m, 9 * j + m + 1)
                at = slice(first + j, first + j + 1)
                buffer[side, row, 0:128] = left[at]
                buffer[side, row, 128 : width - 128] = middle[at]
                buffer[side, row, width - 128 : width] = right[at]
        for a in range(4):
            row = slice(18 + a, 19 + a)
            buffer[side, row, 0:width] = traces[4 * side + a : 4 * side + a + 1, :]
            source = slice(0, 8) if side == 0 else slice(8, 16)
            base = 24 + 2 * a + (0 if side == 0 else 96)
            line = slice(0, 1) if side == 0 else slice(7, 8)
            left = pltpu.roll(from_west[source], (126 - base) % 128, 1)
            right = pltpu.roll(from_east[source], (-base) % 128, 1)
            halo = jnp.where(lane >= 126, left, jnp.where(lane < 2, right, 0.0))
            buffer[side, row, width : width + 128] = halo[line]
    odd_row = lax.rem(lax.axis_index("gy"), 2) == 1
    for j in range(3):
        rows = slice(8 * j, 8 * j + 8)
        low, high = buffer[0, rows, :], buffer[1, rows, :]
        send_even[rows, :] = jnp.where(odd_row, low, high)
        send_odd[rows, :] = jnp.where(odd_row, high, low)


def finish_kernel(width, height, part, swept, fixes, updated, filtered, edges, new, out, tall, sems):
    lane = tile_iota((8, 128), 1)
    tiles = height // 8
    last = slice(width - 128, width)

    for r in range(tiles):
        group, half = r // 2, r % 2
        tile = [fixes[n, 8 * half : 8 * half + 8, :] for n in range(4)]
        rows = slice(8 * r, 8 * r + 8)
        for m in range(9):
            left = jnp.where(lane == 0, turned(tile[2], -32 * group - m, 1), 0.0)
            right = jnp.where(lane == 127, turned(tile[3], 127 - 32 * group - m, 1), 0.0)
            target = edges.at[0 if r == 0 else 1, m] if r in (0, tiles - 1) else new.at[m, rows]
            target[:, 0:128] = part[m, rows, 0:128] + left
            target[:, 128 : width - 128] = part[m, rows, 128 : width - 128]
            target[:, last] = part[m, rows, last] + right
    inner = slice(8, height - 8)
    first_copy = pltpu.make_async_copy(new.at[:, inner], updated.at[:, inner], sems.at[0])
    first_copy.start()

    for r in range(tiles):
        group, half = r // 2, r % 2
        near_w, near_e = (fixes[n, 8 * half : 8 * half + 8, :] for n in range(2))
        rows = slice(8 * r + 8, 8 * r + 16)
        for m in range(9):
            left = jnp.where(lane < 3, turned(near_w, -32 * group - 3 * m, 1), 0.0)
            right = jnp.where(lane >= 125, turned(near_e, 125 - 32 * group - 3 * m, 1), 0.0)
            tall[0, m, rows, :] = swept[m, rows, 0:128] + left
            tall[1, m, rows, :] = swept[m, rows, last] + right
    pad = jnp.zeros((8, 128), F32)
    for side in range(2):
        for m in range(9):
            tall[side, m, 0:8, :] = pad
            tall[side, m, height + 8 : height + 16, :] = pad

    def filtered_copy(a):
        modes = pl.ds(3 * a, 3)
        return pltpu.make_async_copy(out.at[modes, inner], filtered.at[modes, inner], sems.at[1 + a])

    def body(a, carry):
        for r in range(tiles):
            rows = slice(8 * r, 8 * r + 8)
            for cols, source in (
                (slice(0, 128), lambda d, at: tall[0, 3 * a + d, at, :]),
                (slice(128, width - 128), lambda d, at: swept[3 * a + d, at, 128 : width - 128]),
                (last, lambda d, at: tall[1, 3 * a + d, at, :]),
            ):
                def shifted(d, k):
                    return source(d, slice(8 * r + 8 + k, 8 * r + 16 + k))

                for b, value in enumerate(sweep([0, 1, 2], shifted)):
                    if r in (0, tiles - 1):
                        edges[0 if r == 0 else 1, 9 + 3 * a + b, :, cols] = value
                    else:
                        out[3 * a + b, rows, cols] = value
        filtered_copy(a).start()
        return carry

    lax.fori_loop(0, 3, body, 0)
    first_copy.wait()
    for a in range(3):
        filtered_copy(a).wait()


def row_fix_kernel(width, height, got_even, got_odd, sent_even, sent_odd, matrices, edges, updated_in, filtered_in, updated, filtered, tiles, sems):
    odd_row = lax.rem(lax.axis_index("gy"), 2)
    copies = []
    for side in range(2):
        use_odd = lax.rem(side + odd_row, 2) == 0
        got = jnp.where(use_odd, got_odd[...], got_even[...])
        own = jnp.where(use_odd, sent_odd[16:24, :], sent_even[16:24, :])
        edge = got[16:24]
        speed = 0.1 * (edge[5:6] + own[5:6])
        inner, outer = (edge, own) if side == 0 else (own, edge)
        face = jnp.maximum(speed, 0.0) * inner + jnp.minimum(speed, 0.0) * outer
        pieces = [got[:, :width]]
        for k in range(-2, 3):
            pieces.append(turned(face, -k, 1)[:, :width])
        fix = jnp.dot(matrices[side], jnp.concatenate(pieces, axis=0), precision=HIGHEST, preferred_element_type=F32)
        for m in range(9):
            tiles[side, 0, m] = edges[side, m] + fix[72 + 8 * m : 80 + 8 * m]
            tiles[side, 1, m] = edges[side, 9 + m] + fix[8 * m : 8 * m + 8]
        rows = slice(0, 8) if side == 0 else slice(height - 8, height)
        for n, target in enumerate((updated, filtered)):
            copies.append(pltpu.make_async_copy(tiles.at[side, n], target.at[:, rows], sems.at[2 * side + n]))
            copies[-1].start()
    for copy in copies:
        copy.wait()


def swap_pairs(count, offset):
    pairs = []
    for i in range(offset, count + offset, 2):
        one, two = i % count, (i + 1) % count
        pairs += [(one, two), (two, one)]
    return pairs


VMEM = pl.BlockSpec(memory_space=pltpu.VMEM)
HBM = pl.BlockSpec(memory_space=pltpu.HBM)
DMA = pltpu.SemaphoreType.DMA


def call(kernel, out_shape, work, grant=24 << 20, **options):
    return pl.pallas_call(
        kernel,
        out_shape=out_shape,
        compiler_params=pltpu.CompilerParams(vmem_limit_bytes=grant),
        cost_estimate=pl.CostEstimate(flops=work[0], bytes_accessed=work[1], transcendentals=0),
        **options,
    )


def per_device(start_coeffs, section_coeffs, vel_x, vel_y):
    height, width = vel_x.shape
    shape = jax.ShapeDtypeStruct
    full = shape((9, height, width), F32)
    pack = shape((16, 128), F32)
    inputs = (start_coeffs, section_coeffs, vel_x, vel_y)
    west, east, send_odd, send_even = call(
        functools.partial(pack_kernel, width, height),
        (pack,) * 4,
        (20_000_000, 1_400_000),
        grant=62 << 20,
        in_specs=[HBM] * 4,
        out_specs=(VMEM,) * 4,
        scratch_shapes=[
            pltpu.VMEM((2, 9, height, 128), F32),
            pltpu.VMEM((2, 9, height, 128), F32),
            pltpu.VMEM((2, height, 128), F32),
            pltpu.VMEM((2, height, 128), F32),
            pltpu.VMEM((9, height, 128), F32),
            pltpu.VMEM((2, height, 128), F32),
            DMA((8,)),
        ],
    )(*inputs)
    x_odd, x_even = swap_pairs(lax.axis_size("gx"), 1), swap_pairs(lax.axis_size("gx"), 0)
    y_odd, y_even = swap_pairs(lax.axis_size("gy"), 1), swap_pairs(lax.axis_size("gy"), 0)
    got_odd = lax.ppermute(send_odd, "gx", x_odd)
    got_even = lax.ppermute(send_even, "gx", x_even)
    part, swept, traces = call(
        functools.partial(interior_kernel, width, height),
        (full, shape((9, height + 16, width), F32), shape((8, width), F32)),
        (120_000_000, 5_000_000),
        in_specs=[HBM] * 4,
        out_specs=(VMEM,) * 3,
        scratch_shapes=[
            pltpu.VMEM((9, height, width), F32),
            pltpu.VMEM((9, height, width), F32),
            pltpu.VMEM((height, width), F32),
            pltpu.VMEM((height, width), F32),
            pltpu.VMEM((3, height + 8, width), F32),
            DMA((10,)),
        ],
    )(*inputs)
    tall = shape((24, width + 128), F32)
    whole = lambda *dims: pl.BlockSpec(dims, lambda i: (0,) * len(dims))
    send_y_even, send_y_odd, fixes = call(
        functools.partial(edge_kernel, width),
        (tall, tall, shape((4, 16, 128), F32)),
        (4_000_000, 1_000_000),
        grid=(1,),
        in_specs=[whole(16, 128)] * 4
        + [
            pl.BlockSpec((9, 8, width), lambda i: (0, 1, 0)),
            pl.BlockSpec((9, 8, width), lambda i: (0, height // 8, 0)),
            whole(8, width),
            whole(2, 128, 256),
        ],
        out_specs=(whole(24, width + 128), whole(24, width + 128), whole(4, 16, 128)),
        scratch_shapes=[pltpu.VMEM((2, 24, width + 128), F32)],
    )(got_odd, got_even, west, east, swept, swept, traces, jnp.asarray(column_matrices()))
    got_y_even = lax.ppermute(send_y_even, "gy", y_even)
    got_y_odd = lax.ppermute(send_y_odd, "gy", y_odd)
    updated, filtered, edges = call(
        functools.partial(finish_kernel, width, height),
        (full, full, shape((2, 18, 8, width), F32)),
        (60_000_000, 4_000_000),
        in_specs=[VMEM] * 3,
        out_specs=(HBM, HBM, VMEM),
        scratch_shapes=[
            pltpu.VMEM((9, height, width), F32),
            pltpu.VMEM((9, height, width), F32),
            pltpu.VMEM((2, 9, height + 16, 128), F32),
            DMA((4,)),
        ],
    )(part, swept, fixes)
    return call(
        functools.partial(row_fix_kernel, width, height),
        (full, full),
        (4_000_000, 1_000_000),
        in_specs=[VMEM] * 6 + [HBM] * 2,
        out_specs=(HBM, HBM),
        input_output_aliases={6: 0, 7: 1},
        scratch_shapes=[pltpu.VMEM((2, 2, 9, 8, width), F32), DMA((4,))],
    )(got_y_even, got_y_odd, send_y_even, send_y_odd, jnp.asarray(row_matrices()), edges, updated, filtered)


def solution(mesh):
    placed = (P(None, "gy", "gx"), P(None, "gy", "gx"), P("gy", "gx"), P("gy", "gx"))
    return jax.shard_map(
        per_device,
        mesh=mesh,
        in_specs=placed,
        out_specs=(P(None, "gy", "gx"), P(None, "gy", "gx")),
        check_vma=False,
    )
```

```python
import functools

import jax
import jax.numpy as jnp
import numpy as np
from jax import lax
from jax.experimental import pallas as pl
from jax.experimental.pallas import tpu as pltpu
from jax.sharding import PartitionSpec as P


HALF = np.arange(3) + 0.5
PARITY = np.array([1.0, -1.0, 1.0])
GAUSS_NODES = (
    -0.932469514203152,
    -0.6612093864662645,
    -0.2386191860831969,
    0.2386191860831969,
    0.6612093864662645,
    0.932469514203152,
)
GAUSS_WEIGHTS = (
    0.1713244923791704,
    0.3607615730481386,
    0.467913934572691,
    0.467913934572691,
    0.3607615730481386,
    0.1713244923791704,
)
HIGHEST = lax.Precision.HIGHEST
F32 = jnp.float32


def legendre_rows(points):
    return np.stack([points * 0.0 + 1.0, points, 1.5 * points * points - 0.5])


def bspline(points):
    magnitude = np.abs(points)
    return np.where(
        magnitude <= 0.5,
        0.75 - magnitude * magnitude,
        np.where(magnitude <= 1.5, 0.5 * (1.5 - magnitude) ** 2, 0.0),
    )


def kernel_value(points):
    return 1.25 * bspline(points) - 0.125 * (bspline(points + 1.0) + bspline(points - 1.0))


def siac_table():
    nodes = np.array(GAUSS_NODES)
    weights = np.array(GAUSS_WEIGHTS)
    kernel_table = np.zeros((5, 3, 3))
    for slot_index in range(5):
        offset = slot_index - 2
        for low_end, high_end in ((-1.0, 0.0), (0.0, 1.0)):
            for node_value, node_weight in zip(GAUSS_NODES, GAUSS_WEIGHTS):
                xi_value = 0.5 * (low_end + high_end) + 0.5 * (high_end - low_end) * node_value
                outer_weight = 0.5 * (high_end - low_end) * node_weight
                breaks = [-1.0, 1.0]
                for spline_knot in (-2.5, -1.5, -0.5, 0.5, 1.5, 2.5):
                    crossing = xi_value - 2.0 * offset - 2.0 * spline_knot
                    if -1.0 < crossing < 1.0:
                        breaks.append(crossing)
                breaks = sorted(breaks)
                for piece_lo, piece_hi in zip(breaks[:-1], breaks[1:]):
                    eta_points = 0.5 * (piece_lo + piece_hi) + 0.5 * (piece_hi - piece_lo) * nodes
                    eta_weights = 0.5 * (piece_hi - piece_lo) * weights
                    samples = (
                        kernel_value(0.5 * xi_value - 0.5 * eta_points - offset) * eta_weights * 0.5
                    )
                    kernel_table[slot_index] += outer_weight * np.outer(
                        legendre_rows(np.array(xi_value)), legendre_rows(eta_points) @ samples
                    )
    table = kernel_table * (np.arange(3)[None, :, None] + 0.5)
    return table.astype(np.float32).astype(np.float64)


TABLE = siac_table()


def tap(k):
    return TABLE[k + 2] if abs(k) <= 2 else np.zeros((3, 3))


def column_matrices():
    out = np.zeros((2, 128, 256))
    for group in range(4):
        base = 32 * group
        for b in range(3):
            for a in range(3):
                m_out = 3 * a + b
                for i in range(3):
                    col = base + 3 * m_out + i
                    for side, (first, near, far) in enumerate(((-2, -1, 0), (3, 2, 3))):
                        for c in range(3):
                            for j in range(2):
                                out[side, base + 2 * (3 * c + b) + j, col] += tap(first + j - i)[a, c]
                        flux = tap(near - i)[a] @ -HALF + tap(far - i)[a] @ (HALF * PARITY)
                        out[side, base + 18 + b, col] += flux
                out[0, base + 18 + b, 128 + base + m_out] += HALF[a] * PARITY[a]
                out[1, base + 18 + b, 128 + base + m_out] += -HALF[a]
    return out.astype(np.float32)


def row_matrices():
    out = np.zeros((2, 144, 64))
    for a in range(3):
        for b in range(3):
            m_out = 3 * a + b
            for i in range(3):
                for side, (first, near, far, row) in enumerate(((-2, -1, 0, i), (3, 2, 3, 5 + i))):
                    for d in range(3):
                        for j in range(2):
                            out[side, 8 * m_out + row, 9 * j + 3 * a + d] += tap(first + j - i)[b, d]
                    weight = tap(near - i)[b] @ -HALF + tap(far - i)[b] @ (HALF * PARITY)
                    for k in range(-2, 3):
                        for c in range(3):
                            out[side, 8 * m_out + row, 24 + 8 * (k + 2) + 2 + c] += tap(k)[a, c] * weight
            out[0, 72 + 8 * m_out, 24 + 16 + 2 + a] = HALF[b] * PARITY[b]
            out[1, 72 + 8 * m_out + 7, 24 + 16 + 2 + a] = -HALF[b]
    return out.astype(np.float32)


def upwind(speed, inner, outer):
    return jnp.maximum(speed, 0.0) * inner + jnp.minimum(speed, 0.0) * outer


def tile_iota(shape, dim):
    return lax.broadcasted_iota(jnp.int32, shape, dim)


def rows_of(r, count=8, first=0):
    return pl.ds(pl.multiple_of(count * r + first, 8), count)


def turned(value, shift, axis):
    shift %= value.shape[axis]
    return pltpu.roll(value, shift, axis) if shift else value


def update_terms(u, begin, speed_x, speed_y, faces_x, jumps_y):
    sixth_x, sixth_y = 0.6 * speed_x, 0.6 * speed_y
    for b in range(3):
        jump, total = faces_x(b)
        for a in range(3):
            m = 3 * a + b
            value = begin(m) * (1.0 / 3.0) + u[m] * (2.0 / 3.0)
            if a == 0:
                value = value - 0.5 * jump
            elif a == 1:
                value = value + (sixth_x * u[b] - 1.5 * total)
            else:
                value = value + (speed_x * u[3 + b] - 2.5 * jump)
            if b == 0:
                value = value - 0.5 * jumps_y(a, 0)
            elif b == 1:
                value = value + (sixth_y * u[3 * a] - 1.5 * jumps_y(a, 1))
            else:
                value = value + (speed_y * u[3 * a + 1] - 2.5 * jumps_y(a, 0))
            yield m, value


def pack_kernel(width, height, start, sect, vel_x, vel_y, west, east, send_odd, send_even, raw, dense, sems):
    copies = []
    for side in range(2):
        cols = pl.ds(side * (width - 128), 128)
        for n, (source, at) in enumerate(((sect, pl.ds(0, 9)), (start, pl.ds(9, 9)), (vel_x, 18), (vel_y, 19))):
            copies.append(pltpu.make_async_copy(source.at[..., cols], raw.at[side, at], sems.at[4 * side + n]))
            copies[-1].start()
    for copy in copies:
        copy.wait()
    tiles = height // 8
    lane = tile_iota((8, 128), 1)
    sub = tile_iota((8, 128), 0)
    spot = jnp.bitwise_and(lane, 15)

    def gather(m, carry):
        first = acc = None
        for r in range(tiles):
            rows = slice(8 * r, 8 * r + 8)
            moved = turned(jnp.where(lane < 64, raw[0, m, rows, :], raw[1, m, rows, :]), 16 * r, 1)
            if r == 0:
                first = acc = moved
            else:
                acc = jnp.where(lane >= 16 * r - 8, moved, acc)
        acc = jnp.where(lane >= 120, first, acc)
        dense[m] = jnp.where(spot >= 8, pltpu.roll(acc, 16, 1), acc)
        return carry

    lax.fori_loop(0, 20, gather, 0, unroll=4)

    def below(value):
        value = pltpu.roll(value, 1, 0)
        return jnp.where(sub == 0, pltpu.roll(value, 16, 1), value)

    def above(value):
        value = pltpu.roll(value, 7, 0)
        return jnp.where(sub == 7, pltpu.roll(value, 112, 1), value)

    modes = [dense[m] for m in range(9)]
    speed_x, speed_y = dense[18], dense[19]
    speed = jnp.where((sub == 0) & (lane < 16), 0.0, 0.1 * (speed_y + below(speed_y)))
    high, low = jnp.maximum(speed, 0.0), jnp.minimum(speed, 0.0)
    jumps, side_traces = [], []
    for a in range(3):
        even, odd = modes[3 * a] + modes[3 * a + 2], modes[3 * a + 1]
        north, south = even + odd, even - odd
        face = high * below(north) + low * south
        face_north = above(face)
        jumps.append((face_north - face, face_north + face))
        side_traces.append(jnp.where(lane < 64, south, north))
    side_traces.append(speed_y)
    speed = jnp.where(spot == 0, 0.0, 0.1 * (speed_x + pltpu.roll(speed_x, 1, 1)))
    high, low = jnp.maximum(speed, 0.0), jnp.minimum(speed, 0.0)
    column_traces = []

    def faces_x(b):
        even, odd = modes[b] + modes[6 + b], modes[3 + b]
        face = high * pltpu.roll(even + odd, 1, 1) + low * (even - odd)
        beyond = pltpu.roll(face, 127, 1)
        column_traces.append((even - odd, even + odd))
        return beyond - face, beyond + face

    values = dict(
        update_terms(modes, lambda m: dense[9 + m], speed_x, speed_y, faces_x, lambda a, kind: jumps[a][kind])
    )
    odd_column = lax.rem(lax.axis_index("gx"), 2) == 1
    both = []
    for side in range(2):
        two, one = (0, 0) if side == 0 else (14, 15)
        low_slots = turned(values[0], -two, 1)
        for m in range(1, 8):
            low_slots = jnp.where(spot >= 2 * m, turned(values[m], 2 * m - two, 1), low_slots)
        high_slots = turned(values[8], -two, 1)
        singles = [column_traces[b][side] for b in range(3)] + [speed_x] * 3
        for n, value in enumerate(singles):
            high_slots = jnp.where(spot >= 2 + n, turned(value, 2 + n - one, 1), high_slots)
        for n, value in enumerate(side_traces):
            high_slots = jnp.where(spot >= 8 + 2 * n, turned(value, 8 + 2 * n - two, 1), high_slots)
        half = jnp.bitwise_and(lane, 16) == 0
        both.append((
            jnp.where(half, low_slots, pltpu.roll(high_slots, 16, 1)),
            jnp.where(half, pltpu.roll(low_slots, 112, 1), high_slots),
        ))
    for half in range(2):
        rows = slice(8 * half, 8 * half + 8)
        west[rows, :] = both[0][half]
        east[rows, :] = both[1][half]
        send_odd[rows, :] = jnp.where(odd_column, both[1][half], both[0][half])
        send_even[rows, :] = jnp.where(odd_column, both[0][half], both[1][half])


def interior_kernel(
    width, height, start, sect, vel_x, vel_y, updated, filtered, part, swept, traces, edges, s, u, vx, vy, south, new, out, sems
):
    middle = slice(128, width - 128)
    inner = slice(8, height - 8)
    chunk = 16
    tiles = height // 8
    shape = (8, width)
    lane = tile_iota(shape, 1)
    sub = tile_iota(shape, 0)
    pad = jnp.zeros((8, 128), F32)
    nothing = jnp.zeros(shape, F32)

    small = [
        pltpu.make_async_copy(vel_y, vy, sems.at[0]),
        pltpu.make_async_copy(vel_x, vx, sems.at[1]),
    ]
    small[0].start()
    copies = []
    for n in range(height // chunk):
        rows = pl.ds(chunk * n, chunk)
        copies.append(pltpu.make_async_copy(sect.at[:, rows, :], u.at[:, rows, :], sems.at[2 + n]))
        copies[n].start()
    small[1].start()
    begin = []
    for n in range(height // chunk):
        rows = pl.ds(chunk * n, chunk)
        begin.append(pltpu.make_async_copy(start.at[:, rows, :], s.at[:, rows, :], sems.at[2 + height // chunk + n]))
        begin[n].start()

    def south_faces(r, carry):
        rows = rows_of(r)
        speeds = vy[rows, :]
        turned_speed = pltpu.roll(speeds, 1, 0)
        speed = 0.1 * (speeds + jnp.where(sub == 0, carry[3], turned_speed))
        speed = jnp.where((sub == 0) & (r == 0), 0.0, speed)
        high, low = jnp.maximum(speed, 0.0), jnp.minimum(speed, 0.0)
        ahead = []
        for a in range(3):
            even, odd = u[3 * a, rows, :] + u[3 * a + 2, rows, :], u[3 * a + 1, rows, :]
            north = pltpu.roll(even + odd, 1, 0)
            south[a, rows, :] = high * jnp.where(sub == 0, carry[a], north) + low * (even - odd)
            ahead.append(north)
        return (*ahead, turned_speed)

    def shifted(field, k):
        if k == 0:
            return field[:, :width]
        return pltpu.roll(field, (-k) % (width + 128), 1)[:, :width]

    def cells(r, carry):
        rows = rows_of(r)
        after = rows_of(r, first=8)
        modes = [u[m, rows, :] for m in range(9)]
        speed_x, speed_y = vx[rows, :], vy[rows, :]
        speed = jnp.where(lane == 0, 0.0, 0.1 * (speed_x + pltpu.roll(speed_x, 1, 1)))
        high, low = jnp.maximum(speed, 0.0), jnp.minimum(speed, 0.0)
        jump_y, sum_y = [], []
        for a in range(3):
            face = south[a, rows, :]
            above = jnp.where(sub == 7, pltpu.roll(south[a, after, :], 7, 0), pltpu.roll(face, 7, 0))
            jump_y.append(above - face)
            sum_y.append(above + face)

        def faces_x(b):
            even, odd = modes[b] + modes[6 + b], modes[3 + b]
            face = high * pltpu.roll(even + odd, 1, 1) + low * (even - odd)
            beyond = pltpu.roll(face, width - 1, 1)
            return beyond - face, beyond + face

        fields = []
        terms = update_terms(
            modes, lambda m: s[m, rows, :], speed_x, speed_y, faces_x, lambda a, kind: (sum_y if kind else jump_y)[a]
        )
        for m, value in terms:
            part[0, m, rows, :] = value[:, :128]
            new[m, rows, :] = value[:, middle]
            part[1, m, rows, :] = value[:, width - 128 :]
            fields.append(jnp.concatenate([value, pad], axis=1))
            if len(fields) == 3:
                for a, out in enumerate(sweep(fields, shifted)):
                    swept[3 * a + m % 3, after, :] = out
                fields = []
        return carry

    small[0].wait()
    carry = (nothing,) * 4
    for n in range(height // chunk):
        copies[n].wait()
        carry = lax.fori_loop(n * chunk // 8, (n + 1) * chunk // 8, south_faces, carry)
    for a in range(3):
        south[a, height : height + 8, :] = nothing
        even = u[3 * a, 0:8, :] + u[3 * a + 2, 0:8, :]
        traces[a : a + 1, :] = (even - u[3 * a + 1, 0:8, :])[0:1]
        even = u[3 * a, height - 8 :, :] + u[3 * a + 2, height - 8 :, :]
        traces[4 + a : 5 + a, :] = (even + u[3 * a + 1, height - 8 :, :])[7:8]
    traces[3:4, :] = vy[0:1, :]
    traces[7:8, :] = vy[height - 1 :, :]
    for m in range(9):
        swept[m, 0:8, :] = nothing
        swept[m, height + 8 : height + 16, :] = nothing
    small[1].wait()
    for copy in begin:
        copy.wait()
    lax.fori_loop(0, tiles, cells, 0)
    new_copy = pltpu.make_async_copy(new.at[:, inner], updated.at[:, inner, middle], sems.at[10])
    new_copy.start()
    for m in range(9):
        edges[0, m] = new[m, 0:8, :]
        edges[1, m] = new[m, height - 8 :, :]

    def out_copy(a):
        modes = pl.ds(3 * a, 3)
        return pltpu.make_async_copy(out.at[modes, inner], filtered.at[modes, inner, middle], sems.at[11 + a])

    def columns(a, carry):
        for r in range(tiles):

            def taken(d, k):
                return swept[3 * a + d, 8 * r + 8 + k : 8 * r + 16 + k, middle]

            for b, value in enumerate(sweep([0, 1, 2], taken)):
                if r in (0, tiles - 1):
                    edges[0 if r == 0 else 1, 9 + 3 * a + b] = value
                else:
                    out[3 * a + b, 8 * r : 8 * r + 8, :] = value
        out_copy(a).start()
        return carry

    lax.fori_loop(0, 3, columns, 0)
    new_copy.wait()
    for a in range(3):
        out_copy(a).wait()


def sweep(fields, shifted):
    outs = [None, None, None]

    def add(i, term):
        outs[i] = term if outs[i] is None else outs[i] + term

    for c in range(3):
        for a in range(3):
            if TABLE[2, a, c] != 0.0 and (a + c) % 2 == 0:
                add(a, float(TABLE[2, a, c]) * shifted(fields[c], 0))
        for k in (1, 2):
            ahead, behind = shifted(fields[c], k), shifted(fields[c], -k)
            even, odd = ahead + behind, ahead - behind
            for a in range(3):
                add(a, float(TABLE[2 + k, a, c]) * (even if (a + c) % 2 == 0 else odd))
    return outs


def edge_kernel(width, got_odd, got_even, west, east, low_rows, high_rows, traces, matrices, send_even, send_odd, fixes, buffer):
    odd_column = lax.rem(lax.axis_index("gx"), 2) == 1
    from_west = jnp.where(odd_column, got_even[...], got_odd[...])
    from_east = jnp.where(odd_column, got_odd[...], got_even[...])
    lane16 = tile_iota((16, 128), 1)
    place = jnp.bitwise_and(lane16, 31)
    is_face = (place >= 18) & (place < 21)

    def speed_of(one, two):
        return 0.1 * (pltpu.roll(one, 125, 1) + pltpu.roll(two, 125, 1))

    own_w, own_e = west[...], east[...]
    face_w = upwind(speed_of(from_west, own_w), from_west, own_w)
    face_e = upwind(speed_of(from_east, own_e), own_e, from_east)
    fix_w = jnp.dot(jnp.where(is_face, face_w, from_west), matrices[0], precision=HIGHEST, preferred_element_type=F32)
    fix_e = jnp.dot(jnp.where(is_face, face_e, from_east), matrices[1], precision=HIGHEST, preferred_element_type=F32)
    fixes[0] = fix_w[:, :128]
    fixes[1] = fix_e[:, :128]
    fixes[2] = fix_w[:, 128:]
    fixes[3] = fix_e[:, 128:]

    lane = tile_iota((8, 128), 1)
    buffer[...] = jnp.zeros_like(buffer)
    for side, tile in enumerate((low_rows, high_rows)):
        half, turn = (0, 0) if side == 0 else (1, 32)
        first = 0 if side == 0 else 6
        near_w = fix_w[8 * half : 8 * half + 8, :128]
        near_e = fix_e[8 * half : 8 * half + 8, :128]
        for m in range(9):
            turn_w, turn_e = (turn - 3 * m) % 128, (turn + 125 - 3 * m) % 128
            add_w = jnp.where(lane < 3, pltpu.roll(near_w, turn_w, 1) if turn_w else near_w, 0.0)
            add_e = jnp.where(lane >= 125, pltpu.roll(near_e, turn_e, 1) if turn_e else near_e, 0.0)
            left = tile[m, :, :128] + add_w
            right = tile[m, :, width - 128 :] + add_e
            middle = tile[m, :, 128 : width - 128]
            for j in range(2):
                row = slice(9 * j + m, 9 * j + m + 1)
                at = slice(first + j, first + j + 1)
                buffer[side, row, 0:128] = left[at]
                buffer[side, row, 128 : width - 128] = middle[at]
                buffer[side, row, width - 128 : width] = right[at]
        for a in range(4):
            row = slice(18 + a, 19 + a)
            buffer[side, row, 0:width] = traces[4 * side + a : 4 * side + a + 1, :]
            source = slice(0, 8) if side == 0 else slice(8, 16)
            base = 24 + 2 * a + (0 if side == 0 else 96)
            line = slice(0, 1) if side == 0 else slice(7, 8)
            left = pltpu.roll(from_west[source], (126 - base) % 128, 1)
            right = pltpu.roll(from_east[source], (-base) % 128, 1)
            halo = jnp.where(lane >= 126, left, jnp.where(lane < 2, right, 0.0))
            buffer[side, row, width : width + 128] = halo[line]
    odd_row = lax.rem(lax.axis_index("gy"), 2) == 1
    for j in range(3):
        rows = slice(8 * j, 8 * j + 8)
        low, high = buffer[0, rows, :], buffer[1, rows, :]
        send_even[rows, :] = jnp.where(odd_row, low, high)
        send_odd[rows, :] = jnp.where(odd_row, high, low)


def finish_kernel(width, height, part, swept, fixes, updated_in, filtered_in, updated, filtered, edges, new, out, tall, sems):
    lane = tile_iota((8, 128), 1)
    tiles = height // 8
    inner = slice(8, height - 8)
    columns = (slice(0, 128), slice(width - 128, width))
    pad = jnp.zeros((8, 128), F32)
    copies = []
    for side in range(2):
        target = 127 * side
        near = lane < 3 if side == 0 else lane >= 125
        for m in range(9):
            tall[side, m, 0:8, :] = pad
            tall[side, m, height + 8 : height + 16, :] = pad
        for r in range(tiles):
            group, half = r // 2, r % 2
            strip = slice(8 * half, 8 * half + 8)
            rows = slice(8 * r, 8 * r + 8)
            for m in range(9):
                fix = jnp.where(lane == target, turned(fixes[2 + side, strip, :], target - 32 * group - m, 1), 0.0)
                value = part[side, m, rows, :] + fix
                if r in (0, tiles - 1):
                    edges[side, 0 if r == 0 else 1, m] = value
                else:
                    new[side, m, rows, :] = value
                fix = turned(fixes[side, strip, :], 125 * side - 32 * group - 3 * m, 1)
                tall[side, m, 8 * r + 8 : 8 * r + 16, :] = swept[m, 8 * r + 8 : 8 * r + 16, columns[side]] + jnp.where(near, fix, 0.0)
        copies.append(pltpu.make_async_copy(new.at[side, :, inner], updated.at[:, inner, columns[side]], sems.at[side]))
        copies[-1].start()

    def body(a, carry):
        for side in range(2):
            for r in range(tiles):

                def taken(d, k):
                    return tall[side, 3 * a + d, 8 * r + 8 + k : 8 * r + 16 + k, :]

                for b, value in enumerate(sweep([0, 1, 2], taken)):
                    if r in (0, tiles - 1):
                        edges[side, 0 if r == 0 else 1, 9 + 3 * a + b] = value
                    else:
                        out[side, 3 * a + b, 8 * r : 8 * r + 8, :] = value
        return carry

    lax.fori_loop(0, 3, body, 0)
    for side in range(2):
        copies.append(pltpu.make_async_copy(out.at[side, :, inner], filtered.at[:, inner, columns[side]], sems.at[2 + side]))
        copies[-1].start()
    for copy in copies:
        copy.wait()


def row_fix_kernel(width, height, got_even, got_odd, sent_even, sent_odd, matrices, middle, outer, updated_in, filtered_in, updated, filtered, tiles, sems):
    odd_row = lax.rem(lax.axis_index("gy"), 2)
    copies = []
    for side in range(2):
        use_odd = lax.rem(side + odd_row, 2) == 0
        got = jnp.where(use_odd, got_odd[...], got_even[...])
        own = jnp.where(use_odd, sent_odd[16:24, :], sent_even[16:24, :])
        edge = got[16:24]
        speed = 0.1 * (edge[5:6] + own[5:6])
        face = upwind(speed, edge, own) if side == 0 else upwind(speed, own, edge)
        pieces = [got[:, :width]]
        for k in range(-2, 3):
            pieces.append(turned(face, -k, 1)[:, :width])
        fix = jnp.dot(matrices[side], jnp.concatenate(pieces, axis=0), precision=HIGHEST, preferred_element_type=F32)
        for n, first in enumerate((72, 0)):
            for m in range(9):
                add = fix[first + 8 * m : first + 8 * m + 8]
                tiles[side, n, m, :, 0:128] = outer[0, side, 9 * n + m] + add[:, :128]
                tiles[side, n, m, :, 128 : width - 128] = middle[side, 9 * n + m] + add[:, 128 : width - 128]
                tiles[side, n, m, :, width - 128 : width] = outer[1, side, 9 * n + m] + add[:, width - 128 :]
        rows = slice(0, 8) if side == 0 else slice(height - 8, height)
        for n, target in enumerate((updated, filtered)):
            copies.append(pltpu.make_async_copy(tiles.at[side, n], target.at[:, rows], sems.at[2 * side + n]))
            copies[-1].start()
    for copy in copies:
        copy.wait()


def swap_pairs(count, offset):
    pairs = []
    for i in range(offset, count + offset, 2):
        one, two = i % count, (i + 1) % count
        pairs += [(one, two), (two, one)]
    return pairs


VMEM = pl.BlockSpec(memory_space=pltpu.VMEM)
HBM = pl.BlockSpec(memory_space=pltpu.HBM)
DMA = pltpu.SemaphoreType.DMA


def call(kernel, out_shape, work, grant=24 << 20, **options):
    return pl.pallas_call(
        kernel,
        out_shape=out_shape,
        compiler_params=pltpu.CompilerParams(vmem_limit_bytes=grant),
        cost_estimate=pl.CostEstimate(flops=work[0], bytes_accessed=work[1], transcendentals=0),
        **options,
    )


def per_device(start_coeffs, section_coeffs, vel_x, vel_y):
    height, width = vel_x.shape
    shape = jax.ShapeDtypeStruct
    full = shape((9, height, width), F32)
    pack = shape((16, 128), F32)
    inputs = (start_coeffs, section_coeffs, vel_x, vel_y)
    inputs = tuple(pltpu.with_memory_space_constraint(x, pltpu.HBM) for x in inputs)
    west, east, send_odd, send_even = call(
        functools.partial(pack_kernel, width, height),
        (pack,) * 4,
        (20_000_000, 1_400_000),
        in_specs=[HBM] * 4,
        out_specs=(VMEM,) * 4,
        scratch_shapes=[pltpu.VMEM((2, 20, height, 128), F32), pltpu.VMEM((20, 8, 128), F32), DMA((8,))],
    )(*inputs)
    x_odd, x_even = swap_pairs(lax.axis_size("gx"), 1), swap_pairs(lax.axis_size("gx"), 0)
    y_odd, y_even = swap_pairs(lax.axis_size("gy"), 1), swap_pairs(lax.axis_size("gy"), 0)
    got_odd = lax.ppermute(send_odd, "gx", x_odd)
    got_even = lax.ppermute(send_even, "gx", x_even)
    updated, filtered, part, swept, traces, middle = call(
        functools.partial(interior_kernel, width, height),
        (
            full,
            full,
            shape((2, 9, height, 128), F32),
            shape((9, height + 16, width), F32),
            shape((8, width), F32),
            shape((2, 18, 8, width - 256), F32),
        ),
        (120_000_000, 5_000_000),
        in_specs=[HBM] * 4,
        out_specs=(HBM, HBM) + (VMEM,) * 4,
        scratch_shapes=[
            pltpu.VMEM((9, height, width), F32),
            pltpu.VMEM((9, height, width), F32),
            pltpu.VMEM((height, width), F32),
            pltpu.VMEM((height, width), F32),
            pltpu.VMEM((3, height + 8, width), F32),
            pltpu.VMEM((9, height, width - 256), F32),
            pltpu.VMEM((9, height, width - 256), F32),
            DMA((14,)),
        ],
    )(*inputs)
    tall = shape((24, width + 128), F32)
    whole = lambda *dims: pl.BlockSpec(dims, lambda i: (0,) * len(dims))
    send_y_even, send_y_odd, fixes = call(
        functools.partial(edge_kernel, width),
        (tall, tall, shape((4, 16, 128), F32)),
        (4_000_000, 1_000_000),
        grid=(1,),
        in_specs=[whole(16, 128)] * 4
        + [
            pl.BlockSpec((9, 8, width), lambda i: (0, 1, 0)),
            pl.BlockSpec((9, 8, width), lambda i: (0, height // 8, 0)),
            whole(8, width),
            whole(2, 128, 256),
        ],
        out_specs=(whole(24, width + 128), whole(24, width + 128), whole(4, 16, 128)),
        scratch_shapes=[pltpu.VMEM((2, 24, width + 128), F32)],
    )(got_odd, got_even, west, east, swept, swept, traces, jnp.asarray(column_matrices()))
    got_y_even = lax.ppermute(send_y_even, "gy", y_even)
    got_y_odd = lax.ppermute(send_y_odd, "gy", y_odd)
    updated, filtered, outer = call(
        functools.partial(finish_kernel, width, height),
        (full, full, shape((2, 2, 18, 8, 128), F32)),
        (60_000_000, 4_000_000),
        in_specs=[VMEM] * 3 + [HBM] * 2,
        out_specs=(HBM, HBM, VMEM),
        input_output_aliases={3: 0, 4: 1},
        scratch_shapes=[
            pltpu.VMEM((2, 9, height, 128), F32),
            pltpu.VMEM((2, 9, height, 128), F32),
            pltpu.VMEM((2, 9, height + 16, 128), F32),
            DMA((4,)),
        ],
    )(part, swept, fixes, updated, filtered)
    return call(
        functools.partial(row_fix_kernel, width, height),
        (full, full),
        (4_000_000, 1_000_000),
        in_specs=[VMEM] * 7 + [HBM] * 2,
        out_specs=(HBM, HBM),
        input_output_aliases={7: 0, 8: 1},
        scratch_shapes=[pltpu.VMEM((2, 2, 9, 8, width), F32), DMA((4,))],
    )(got_y_even, got_y_odd, send_y_even, send_y_odd, jnp.asarray(row_matrices()), middle, outer, updated, filtered)


def solution(mesh):
    placed = (P(None, "gy", "gx"), P(None, "gy", "gx"), P("gy", "gx"), P("gy", "gx"))
    return jax.shard_map(
        per_device,
        mesh=mesh,
        in_specs=placed,
        out_specs=(P(None, "gy", "gx"), P(None, "gy", "gx")),
        check_vma=False,
    )
```

```python
import functools

import jax
import jax.numpy as jnp
import numpy as np
from jax import lax
from jax.experimental import pallas as pl
from jax.experimental.pallas import tpu as pltpu
from jax.sharding import PartitionSpec as P


HALF = np.arange(3) + 0.5
PARITY = np.array([1.0, -1.0, 1.0])
GAUSS_NODES = (
    -0.932469514203152,
    -0.6612093864662645,
    -0.2386191860831969,
    0.2386191860831969,
    0.6612093864662645,
    0.932469514203152,
)
GAUSS_WEIGHTS = (
    0.1713244923791704,
    0.3607615730481386,
    0.467913934572691,
    0.467913934572691,
    0.3607615730481386,
    0.1713244923791704,
)
HIGHEST = lax.Precision.HIGHEST
F32 = jnp.float32


def legendre_rows(points):
    return np.stack([points * 0.0 + 1.0, points, 1.5 * points * points - 0.5])


def bspline(points):
    magnitude = np.abs(points)
    return np.where(
        magnitude <= 0.5,
        0.75 - magnitude * magnitude,
        np.where(magnitude <= 1.5, 0.5 * (1.5 - magnitude) ** 2, 0.0),
    )


def kernel_value(points):
    return 1.25 * bspline(points) - 0.125 * (bspline(points + 1.0) + bspline(points - 1.0))


def siac_table():
    nodes = np.array(GAUSS_NODES)
    weights = np.array(GAUSS_WEIGHTS)
    kernel_table = np.zeros((5, 3, 3))
    for slot_index in range(5):
        offset = slot_index - 2
        for low_end, high_end in ((-1.0, 0.0), (0.0, 1.0)):
            for node_value, node_weight in zip(GAUSS_NODES, GAUSS_WEIGHTS):
                xi_value = 0.5 * (low_end + high_end) + 0.5 * (high_end - low_end) * node_value
                outer_weight = 0.5 * (high_end - low_end) * node_weight
                breaks = [-1.0, 1.0]
                for spline_knot in (-2.5, -1.5, -0.5, 0.5, 1.5, 2.5):
                    crossing = xi_value - 2.0 * offset - 2.0 * spline_knot
                    if -1.0 < crossing < 1.0:
                        breaks.append(crossing)
                breaks = sorted(breaks)
                for piece_lo, piece_hi in zip(breaks[:-1], breaks[1:]):
                    eta_points = 0.5 * (piece_lo + piece_hi) + 0.5 * (piece_hi - piece_lo) * nodes
                    eta_weights = 0.5 * (piece_hi - piece_lo) * weights
                    samples = (
                        kernel_value(0.5 * xi_value - 0.5 * eta_points - offset) * eta_weights * 0.5
                    )
                    kernel_table[slot_index] += outer_weight * np.outer(
                        legendre_rows(np.array(xi_value)), legendre_rows(eta_points) @ samples
                    )
    table = kernel_table * (np.arange(3)[None, :, None] + 0.5)
    return table.astype(np.float32).astype(np.float64)


TABLE = siac_table()


def tap(k):
    return TABLE[k + 2] if abs(k) <= 2 else np.zeros((3, 3))


def column_matrices():
    out = np.zeros((2, 128, 256))
    for group in range(4):
        base = 32 * group
        for b in range(3):
            for a in range(3):
                m_out = 3 * a + b
                for i in range(3):
                    col = base + 3 * m_out + i
                    for side, (first, near, far) in enumerate(((-2, -1, 0), (3, 2, 3))):
                        for c in range(3):
                            for j in range(2):
                                out[side, base + 2 * (3 * c + b) + j, col] += tap(first + j - i)[a, c]
                        flux = tap(near - i)[a] @ -HALF + tap(far - i)[a] @ (HALF * PARITY)
                        out[side, base + 18 + b, col] += flux
                out[0, base + 18 + b, 128 + base + m_out] += HALF[a] * PARITY[a]
                out[1, base + 18 + b, 128 + base + m_out] += -HALF[a]
    return out.astype(np.float32)


def row_matrices():
    out = np.zeros((2, 144, 64))
    for a in range(3):
        for b in range(3):
            m_out = 3 * a + b
            for i in range(3):
                for side, (first, near, far, row) in enumerate(((-2, -1, 0, i), (3, 2, 3, 5 + i))):
                    for d in range(3):
                        for j in range(2):
                            out[side, 8 * m_out + row, 9 * j + 3 * a + d] += tap(first + j - i)[b, d]
                    weight = tap(near - i)[b] @ -HALF + tap(far - i)[b] @ (HALF * PARITY)
                    for k in range(-2, 3):
                        for c in range(3):
                            out[side, 8 * m_out + row, 24 + 8 * (k + 2) + 2 + c] += tap(k)[a, c] * weight
            out[0, 72 + 8 * m_out, 24 + 16 + 2 + a] = HALF[b] * PARITY[b]
            out[1, 72 + 8 * m_out + 7, 24 + 16 + 2 + a] = -HALF[b]
    return out.astype(np.float32)


def upwind(speed, inner, outer):
    return jnp.maximum(speed, 0.0) * inner + jnp.minimum(speed, 0.0) * outer


def tile_iota(shape, dim):
    return lax.broadcasted_iota(jnp.int32, shape, dim)


def rows_of(r, count=8, first=0):
    return pl.ds(pl.multiple_of(count * r + first, 8), count)


def turned(value, shift, axis):
    shift %= value.shape[axis]
    return pltpu.roll(value, shift, axis) if shift else value


def update_terms(u, begin, speed_x, speed_y, faces_x, jumps_y):
    sixth_x, sixth_y = 0.6 * speed_x, 0.6 * speed_y
    for b in range(3):
        jump, total = faces_x(b)
        for a in range(3):
            m = 3 * a + b
            value = begin(m) * (1.0 / 3.0) + u[m] * (2.0 / 3.0)
            if a == 0:
                value = value - 0.5 * jump
            elif a == 1:
                value = value + (sixth_x * u[b] - 1.5 * total)
            else:
                value = value + (speed_x * u[3 + b] - 2.5 * jump)
            if b == 0:
                value = value - 0.5 * jumps_y(a, 0)
            elif b == 1:
                value = value + (sixth_y * u[3 * a] - 1.5 * jumps_y(a, 1))
            else:
                value = value + (speed_y * u[3 * a + 1] - 2.5 * jumps_y(a, 0))
            yield m, value


def pack_kernel(width, height, start, sect, vel_x, vel_y, west, east, send_odd, send_even, raw, dense, sems):
    copies = []
    for n, (source, at) in enumerate(((sect, pl.ds(0, 9)), (vel_x, 9), (vel_y, 10), (start, pl.ds(11, 9)))):
        for side in range(2):
            cols = pl.ds(side * (width - 128), 128)
            copies.append(pltpu.make_async_copy(source.at[..., cols], raw.at[side, at], sems.at[2 * n + side]))
            copies[-1].start()
    tiles = height // 8
    lane = tile_iota((8, 128), 1)
    sub = tile_iota((8, 128), 0)
    spot = jnp.bitwise_and(lane, 15)

    def gather(m, carry):
        first = acc = None
        for r in range(tiles):
            rows = slice(8 * r, 8 * r + 8)
            moved = turned(jnp.where(lane < 64, raw[0, m, rows, :], raw[1, m, rows, :]), 16 * r, 1)
            if r == 0:
                first = acc = moved
            else:
                acc = jnp.where(lane >= 16 * r - 8, moved, acc)
        acc = jnp.where(lane >= 120, first, acc)
        dense[m] = jnp.where(spot >= 8, pltpu.roll(acc, 16, 1), acc)
        return carry

    for copy in copies[:2]:
        copy.wait()
    lax.fori_loop(0, 9, gather, 0, unroll=3)
    for copy in copies[2:]:
        copy.wait()
    lax.fori_loop(9, 20, gather, 0, unroll=4)

    def below(value):
        value = pltpu.roll(value, 1, 0)
        return jnp.where(sub == 0, pltpu.roll(value, 16, 1), value)

    def above(value):
        value = pltpu.roll(value, 7, 0)
        return jnp.where(sub == 7, pltpu.roll(value, 112, 1), value)

    modes = [dense[m] for m in range(9)]
    speed_x, speed_y = dense[9], dense[10]
    speed = jnp.where((sub == 0) & (lane < 16), 0.0, 0.1 * (speed_y + below(speed_y)))
    high, low = jnp.maximum(speed, 0.0), jnp.minimum(speed, 0.0)
    jumps, side_traces = [], []
    for a in range(3):
        even, odd = modes[3 * a] + modes[3 * a + 2], modes[3 * a + 1]
        north, south = even + odd, even - odd
        face = high * below(north) + low * south
        face_north = above(face)
        jumps.append((face_north - face, face_north + face))
        side_traces.append(jnp.where(lane < 64, south, north))
    side_traces.append(speed_y)
    speed = jnp.where(spot == 0, 0.0, 0.1 * (speed_x + pltpu.roll(speed_x, 1, 1)))
    high, low = jnp.maximum(speed, 0.0), jnp.minimum(speed, 0.0)
    column_traces = []

    def faces_x(b):
        even, odd = modes[b] + modes[6 + b], modes[3 + b]
        face = high * pltpu.roll(even + odd, 1, 1) + low * (even - odd)
        beyond = pltpu.roll(face, 127, 1)
        column_traces.append((even - odd, even + odd))
        return beyond - face, beyond + face

    values = dict(
        update_terms(modes, lambda m: dense[11 + m], speed_x, speed_y, faces_x, lambda a, kind: jumps[a][kind])
    )
    odd_column = lax.rem(lax.axis_index("gx"), 2) == 1
    both = []
    for side in range(2):
        two, one = (0, 0) if side == 0 else (14, 15)
        low_slots = turned(values[0], -two, 1)
        for m in range(1, 8):
            low_slots = jnp.where(spot >= 2 * m, turned(values[m], 2 * m - two, 1), low_slots)
        high_slots = turned(values[8], -two, 1)
        singles = [column_traces[b][side] for b in range(3)] + [speed_x] * 3
        for n, value in enumerate(singles):
            high_slots = jnp.where(spot >= 2 + n, turned(value, 2 + n - one, 1), high_slots)
        for n, value in enumerate(side_traces):
            high_slots = jnp.where(spot >= 8 + 2 * n, turned(value, 8 + 2 * n - two, 1), high_slots)
        half = jnp.bitwise_and(lane, 16) == 0
        both.append((
            jnp.where(half, low_slots, pltpu.roll(high_slots, 16, 1)),
            jnp.where(half, pltpu.roll(low_slots, 112, 1), high_slots),
        ))
    for half in range(2):
        rows = slice(8 * half, 8 * half + 8)
        west[rows, :] = both[0][half]
        east[rows, :] = both[1][half]
        send_odd[rows, :] = jnp.where(odd_column, both[1][half], both[0][half])
        send_even[rows, :] = jnp.where(odd_column, both[0][half], both[1][half])


def sweep_rows(tiles, load, store):
    sub = tile_iota((8, 128), 0)
    cache = {}

    def rolled(d, r, amount):
        if not 0 <= r < tiles:
            return 0.0
        if (d, r, amount) not in cache:
            cache[d, r, amount] = turned(load(d, r), amount, 0)
        return cache[d, r, amount]

    for r in range(tiles):

        def taken(d, k):
            if k == 0:
                return rolled(d, r, 0)
            if k > 0:
                return jnp.where(sub < 8 - k, rolled(d, r, 8 - k), rolled(d, r + 1, 8 - k))
            return jnp.where(sub >= -k, rolled(d, r, -k), rolled(d, r - 1, -k))

        for b, value in enumerate(sweep([0, 1, 2], taken)):
            store(b, r, value)


def interior_kernel(width, height, early, *refs):
    inputs, rest = refs[:4], refs[4 if early else 10 :]

    @pl.when((lax.axis_index("gx") == 0) == early)
    def _():
        interior(width, height, *inputs, *rest)


def interior(
    width, height, start, sect, vel_x, vel_y, updated, filtered, part, swept, traces, edges, s, u, vx, vy, south, new, out, sems
):
    middle = slice(128, width - 128)
    inner = slice(8, height - 8)
    chunk = 16
    tiles = height // 8
    shape = (8, width)
    lane = tile_iota(shape, 1)
    sub = tile_iota(shape, 0)
    nothing = jnp.zeros(shape, F32)

    small = [
        pltpu.make_async_copy(vel_y, vy, sems.at[0]),
        pltpu.make_async_copy(vel_x, vx, sems.at[1]),
    ]
    small[0].start()
    copies = []
    for n in range(height // chunk):
        rows = pl.ds(chunk * n, chunk)
        copies.append(pltpu.make_async_copy(sect.at[:, rows, :], u.at[:, rows, :], sems.at[2 + n]))
        copies[n].start()
    small[1].start()
    begin = []
    for n in range(height // chunk):
        rows = pl.ds(chunk * n, chunk)
        begin.append(pltpu.make_async_copy(start.at[:, rows, :], s.at[:, rows, :], sems.at[2 + height // chunk + n]))
        begin[n].start()

    def south_faces(r, carry):
        rows = rows_of(r)
        speeds = vy[rows, :]
        turned_speed = pltpu.roll(speeds, 1, 0)
        speed = 0.1 * (speeds + jnp.where(sub == 0, carry[3], turned_speed))
        speed = jnp.where((sub == 0) & (r == 0), 0.0, speed)
        high, low = jnp.maximum(speed, 0.0), jnp.minimum(speed, 0.0)
        ahead = []
        for a in range(3):
            even, odd = u[3 * a, rows, :] + u[3 * a + 2, rows, :], u[3 * a + 1, rows, :]
            north = pltpu.roll(even + odd, 1, 0)
            south[a, rows, :] = high * jnp.where(sub == 0, carry[a], north) + low * (even - odd)
            ahead.append(north)
        return (*ahead, turned_speed)

    pieces = width // 128
    narrow = tile_iota((8, 128), 1)

    def sweep_columns(fields, store):
        cache = {}

        def rolled(c, j, amount):
            if not 0 <= j < pieces:
                return 0.0
            if (c, j, amount) not in cache:
                cache[c, j, amount] = turned(fields[c][:, 128 * j : 128 * j + 128], amount, 1)
            return cache[c, j, amount]

        for j in range(pieces):

            def taken(c, k):
                if k == 0:
                    return rolled(c, j, 0)
                if k > 0:
                    return jnp.where(narrow < 128 - k, rolled(c, j, 128 - k), rolled(c, j + 1, 128 - k))
                return jnp.where(narrow >= -k, rolled(c, j, -k), rolled(c, j - 1, -k))

            for a, value in enumerate(sweep([0, 1, 2], taken)):
                store(a, slice(128 * j, 128 * j + 128), value)

    def cells(r, carry):
        rows = rows_of(r)
        after = rows_of(r, first=8)
        modes = [u[m, rows, :] for m in range(9)]
        speed_x, speed_y = vx[rows, :], vy[rows, :]
        speed = jnp.where(lane == 0, 0.0, 0.1 * (speed_x + pltpu.roll(speed_x, 1, 1)))
        high, low = jnp.maximum(speed, 0.0), jnp.minimum(speed, 0.0)
        jump_y, sum_y = [], []
        for a in range(3):
            face = south[a, rows, :]
            above = jnp.where(sub == 7, pltpu.roll(south[a, after, :], 7, 0), pltpu.roll(face, 7, 0))
            jump_y.append(above - face)
            sum_y.append(above + face)

        def faces_x(b):
            even, odd = modes[b] + modes[6 + b], modes[3 + b]
            face = high * pltpu.roll(even + odd, 1, 1) + low * (even - odd)
            beyond = pltpu.roll(face, width - 1, 1)
            return beyond - face, beyond + face

        fields = []
        terms = update_terms(
            modes, lambda m: s[m, rows, :], speed_x, speed_y, faces_x, lambda a, kind: (sum_y if kind else jump_y)[a]
        )
        for m, value in terms:
            part[0, m, rows, :] = value[:, :128]
            new[m, rows, :] = value[:, middle]
            part[1, m, rows, :] = value[:, width - 128 :]
            fields.append(value)
            if len(fields) == 3:

                def keep(a, cols, value, b=m % 3):
                    swept[3 * a + b, rows, cols] = value

                sweep_columns(fields, keep)
                fields = []
        return carry

    small[0].wait()
    carry = (nothing,) * 4
    for n in range(height // chunk):
        copies[n].wait()
        carry = lax.fori_loop(n * chunk // 8, (n + 1) * chunk // 8, south_faces, carry)
    for a in range(3):
        south[a, height : height + 8, :] = nothing
        even = u[3 * a, 0:8, :] + u[3 * a + 2, 0:8, :]
        traces[a : a + 1, :] = (even - u[3 * a + 1, 0:8, :])[0:1]
        even = u[3 * a, height - 8 :, :] + u[3 * a + 2, height - 8 :, :]
        traces[4 + a : 5 + a, :] = (even + u[3 * a + 1, height - 8 :, :])[7:8]
    traces[3:4, :] = vy[0:1, :]
    traces[7:8, :] = vy[height - 1 :, :]
    small[1].wait()
    for n in range(height // chunk):
        begin[n].wait()
        lax.fori_loop(n * chunk // 8, (n + 1) * chunk // 8, cells, 0)
    new_copy = pltpu.make_async_copy(new.at[:, inner], updated.at[:, inner, middle], sems.at[10])
    new_copy.start()
    for m in range(9):
        edges[0, m] = new[m, 0:8, :]
        edges[1, m] = new[m, height - 8 :, :]

    def out_copy(a):
        modes = pl.ds(3 * a, 3)
        return pltpu.make_async_copy(out.at[modes, inner], filtered.at[modes, inner, middle], sems.at[11 + a])

    def columns(a, carry):
        def column(j, carry):
            source = pl.ds(pl.multiple_of(128 * j + 128, 128), 128)
            target = pl.ds(pl.multiple_of(128 * j, 128), 128)

            def store(b, r, value):
                if r in (0, tiles - 1):
                    edges[0 if r == 0 else 1, 9 + 3 * a + b, :, target] = value
                else:
                    out[3 * a + b, 8 * r : 8 * r + 8, target] = value

            sweep_rows(tiles, lambda d, r: swept[3 * a + d, 8 * r : 8 * r + 8, source], store)
            return carry

        lax.fori_loop(0, pieces - 2, column, 0)
        out_copy(a).start()
        return carry

    lax.fori_loop(0, 3, columns, 0)
    new_copy.wait()
    for a in range(3):
        out_copy(a).wait()


def sweep(fields, shifted):
    outs = [None, None, None]

    def add(i, term):
        outs[i] = term if outs[i] is None else outs[i] + term

    for c in range(3):
        for a in range(3):
            if TABLE[2, a, c] != 0.0 and (a + c) % 2 == 0:
                add(a, float(TABLE[2, a, c]) * shifted(fields[c], 0))
        for k in (1, 2):
            ahead, behind = shifted(fields[c], k), shifted(fields[c], -k)
            even, odd = ahead + behind, ahead - behind
            for a in range(3):
                add(a, float(TABLE[2 + k, a, c]) * (even if (a + c) % 2 == 0 else odd))
    return outs


def edge_kernel(width, got_odd, got_even, west, east, low_rows, high_rows, traces, matrices, send_even, send_odd, fixes, buffer):
    odd_column = lax.rem(lax.axis_index("gx"), 2) == 1
    from_west = jnp.where(odd_column, got_even[...], got_odd[...])
    from_east = jnp.where(odd_column, got_odd[...], got_even[...])
    lane16 = tile_iota((16, 128), 1)
    place = jnp.bitwise_and(lane16, 31)
    is_face = (place >= 18) & (place < 21)

    def speed_of(one, two):
        return 0.1 * (pltpu.roll(one, 125, 1) + pltpu.roll(two, 125, 1))

    own_w, own_e = west[...], east[...]
    face_w = upwind(speed_of(from_west, own_w), from_west, own_w)
    face_e = upwind(speed_of(from_east, own_e), own_e, from_east)
    fix_w = jnp.dot(jnp.where(is_face, face_w, from_west), matrices[0], precision=HIGHEST, preferred_element_type=F32)
    fix_e = jnp.dot(jnp.where(is_face, face_e, from_east), matrices[1], precision=HIGHEST, preferred_element_type=F32)
    fixes[0] = fix_w[:, :128]
    fixes[1] = fix_e[:, :128]
    fixes[2] = fix_w[:, 128:]
    fixes[3] = fix_e[:, 128:]

    lane = tile_iota((8, 128), 1)
    buffer[...] = jnp.zeros_like(buffer)
    for side, tile in enumerate((low_rows, high_rows)):
        half, turn = (0, 0) if side == 0 else (1, 32)
        first = 0 if side == 0 else 6
        near_w = fix_w[8 * half : 8 * half + 8, :128]
        near_e = fix_e[8 * half : 8 * half + 8, :128]
        for m in range(9):
            turn_w, turn_e = (turn - 3 * m) % 128, (turn + 125 - 3 * m) % 128
            add_w = jnp.where(lane < 3, pltpu.roll(near_w, turn_w, 1) if turn_w else near_w, 0.0)
            add_e = jnp.where(lane >= 125, pltpu.roll(near_e, turn_e, 1) if turn_e else near_e, 0.0)
            left = tile[m, :, :128] + add_w
            right = tile[m, :, width - 128 :] + add_e
            middle = tile[m, :, 128 : width - 128]
            for j in range(2):
                row = slice(9 * j + m, 9 * j + m + 1)
                at = slice(first + j, first + j + 1)
                buffer[side, row, 0:128] = left[at]
                buffer[side, row, 128 : width - 128] = middle[at]
                buffer[side, row, width - 128 : width] = right[at]
        for a in range(4):
            row = slice(18 + a, 19 + a)
            buffer[side, row, 0:width] = traces[4 * side + a : 4 * side + a + 1, :]
            source = slice(0, 8) if side == 0 else slice(8, 16)
            base = 24 + 2 * a + (0 if side == 0 else 96)
            line = slice(0, 1) if side == 0 else slice(7, 8)
            left = pltpu.roll(from_west[source], (126 - base) % 128, 1)
            right = pltpu.roll(from_east[source], (-base) % 128, 1)
            halo = jnp.where(lane >= 126, left, jnp.where(lane < 2, right, 0.0))
            buffer[side, row, width : width + 128] = halo[line]
    odd_row = lax.rem(lax.axis_index("gy"), 2) == 1
    for j in range(3):
        rows = slice(8 * j, 8 * j + 8)
        low, high = buffer[0, rows, :], buffer[1, rows, :]
        send_even[rows, :] = jnp.where(odd_row, low, high)
        send_odd[rows, :] = jnp.where(odd_row, high, low)


def finish_kernel(width, height, part, swept, fixes, updated_in, filtered_in, updated, filtered, edges, new, out, tall, sems):
    lane = tile_iota((8, 128), 1)
    tiles = height // 8
    inner = slice(8, height - 8)
    columns = (slice(0, 128), slice(width - 128, width))
    copies = []
    for side in range(2):
        target = 127 * side
        near = lane < 3 if side == 0 else lane >= 125
        for r in range(tiles):
            group, half = r // 2, r % 2
            strip = slice(8 * half, 8 * half + 8)
            rows = slice(8 * r, 8 * r + 8)
            for m in range(9):
                fix = jnp.where(lane == target, turned(fixes[2 + side, strip, :], target - 32 * group - m, 1), 0.0)
                value = part[side, m, rows, :] + fix
                if r in (0, tiles - 1):
                    edges[side, 0 if r == 0 else 1, m] = value
                else:
                    new[side, m, rows, :] = value
                fix = turned(fixes[side, strip, :], 125 * side - 32 * group - 3 * m, 1)
                tall[side, m, rows, :] = swept[m, rows, columns[side]] + jnp.where(near, fix, 0.0)
        copies.append(pltpu.make_async_copy(new.at[side, :, inner], updated.at[:, inner, columns[side]], sems.at[side]))
        copies[-1].start()

    for side in range(2):

        def body(a, carry, side=side):
            def store(b, r, value):
                if r in (0, tiles - 1):
                    edges[side, 0 if r == 0 else 1, 9 + 3 * a + b] = value
                else:
                    out[side, 3 * a + b, 8 * r : 8 * r + 8, :] = value

            sweep_rows(tiles, lambda d, r: tall[side, 3 * a + d, 8 * r : 8 * r + 8, :], store)
            return carry

        lax.fori_loop(0, 3, body, 0)
        copies.append(pltpu.make_async_copy(out.at[side, :, inner], filtered.at[:, inner, columns[side]], sems.at[2 + side]))
        copies[-1].start()
    for copy in copies:
        copy.wait()


def row_fix_kernel(width, height, got_even, got_odd, sent_even, sent_odd, matrices, middle, outer, updated_in, filtered_in, updated, filtered, tiles, sems):
    odd_row = lax.rem(lax.axis_index("gy"), 2)
    copies = []
    for side in range(2):
        use_odd = lax.rem(side + odd_row, 2) == 0
        got = jnp.where(use_odd, got_odd[...], got_even[...])
        own = jnp.where(use_odd, sent_odd[16:24, :], sent_even[16:24, :])
        edge = got[16:24]
        speed = 0.1 * (edge[5:6] + own[5:6])
        face = upwind(speed, edge, own) if side == 0 else upwind(speed, own, edge)
        pieces = [got[:, :width]]
        for k in range(-2, 3):
            pieces.append(turned(face, -k, 1)[:, :width])
        fix = jnp.dot(matrices[side], jnp.concatenate(pieces, axis=0), precision=HIGHEST, preferred_element_type=F32)
        for n, first in enumerate((72, 0)):
            for m in range(9):
                add = fix[first + 8 * m : first + 8 * m + 8]
                tiles[side, n, m, :, 0:128] = outer[0, side, 9 * n + m] + add[:, :128]
                tiles[side, n, m, :, 128 : width - 128] = middle[side, 9 * n + m] + add[:, 128 : width - 128]
                tiles[side, n, m, :, width - 128 : width] = outer[1, side, 9 * n + m] + add[:, width - 128 :]
        rows = slice(0, 8) if side == 0 else slice(height - 8, height)
        for n, target in enumerate((updated, filtered)):
            copies.append(pltpu.make_async_copy(tiles.at[side, n], target.at[:, rows], sems.at[2 * side + n]))
            copies[-1].start()
    for copy in copies:
        copy.wait()


def swap_pairs(count, offset):
    pairs = []
    for i in range(offset, count + offset, 2):
        one, two = i % count, (i + 1) % count
        pairs += [(one, two), (two, one)]
    return pairs


VMEM = pl.BlockSpec(memory_space=pltpu.VMEM)
HBM = pl.BlockSpec(memory_space=pltpu.HBM)
DMA = pltpu.SemaphoreType.DMA


def call(kernel, out_shape, work, grant=24 << 20, **options):
    return pl.pallas_call(
        kernel,
        out_shape=out_shape,
        compiler_params=pltpu.CompilerParams(vmem_limit_bytes=grant),
        cost_estimate=pl.CostEstimate(flops=work[0], bytes_accessed=work[1], transcendentals=0),
        **options,
    )


def per_device(start_coeffs, section_coeffs, vel_x, vel_y):
    height, width = vel_x.shape
    shape = jax.ShapeDtypeStruct
    full = shape((9, height, width), F32)
    pack = shape((16, 128), F32)
    inputs = (start_coeffs, section_coeffs, vel_x, vel_y)
    inputs = tuple(pltpu.with_memory_space_constraint(x, pltpu.HBM) for x in inputs)
    west, east, send_odd, send_even = call(
        functools.partial(pack_kernel, width, height),
        (pack,) * 4,
        (20_000_000, 1_400_000),
        in_specs=[HBM] * 4,
        out_specs=(VMEM,) * 4,
        scratch_shapes=[pltpu.VMEM((2, 20, height, 128), F32), pltpu.VMEM((20, 8, 128), F32), DMA((8,))],
    )(*inputs)
    x_odd, x_even = swap_pairs(lax.axis_size("gx"), 1), swap_pairs(lax.axis_size("gx"), 0)
    y_odd, y_even = swap_pairs(lax.axis_size("gy"), 1), swap_pairs(lax.axis_size("gy"), 0)
    got_even = lax.ppermute(send_even, "gx", x_even)
    got_odd = lax.ppermute(send_odd, "gx", x_odd)
    local = (
        full,
        full,
        shape((2, 9, height, 128), F32),
        full,
        shape((8, width), F32),
        shape((2, 18, 8, width - 256), F32),
    )
    made = ()
    for early in (True, False):
        made = call(
            functools.partial(interior_kernel, width, height, early),
            local,
            (120_000_000, 5_000_000),
            in_specs=[HBM] * 4 + ([] if early else [HBM] * 2 + [VMEM] * 4),
            out_specs=(HBM, HBM) + (VMEM,) * 4,
            input_output_aliases={} if early else {4 + n: n for n in range(6)},
            scratch_shapes=[
                pltpu.VMEM((9, height, width), F32),
                pltpu.VMEM((9, height, width), F32),
                pltpu.VMEM((height, width), F32),
                pltpu.VMEM((height, width), F32),
                pltpu.VMEM((3, height + 8, width), F32),
                pltpu.VMEM((9, height, width - 256), F32),
                pltpu.VMEM((9, height, width - 256), F32),
                DMA((14,)),
            ],
        )(*inputs, *made)
    updated, filtered, part, swept, traces, middle = made
    tall = shape((24, width + 128), F32)
    whole = lambda *dims: pl.BlockSpec(dims, lambda i: (0,) * len(dims))
    send_y_even, send_y_odd, fixes = call(
        functools.partial(edge_kernel, width),
        (tall, tall, shape((4, 16, 128), F32)),
        (4_000_000, 1_000_000),
        grid=(1,),
        in_specs=[whole(16, 128)] * 4
        + [
            pl.BlockSpec((9, 8, width), lambda i: (0, 0, 0)),
            pl.BlockSpec((9, 8, width), lambda i: (0, height // 8 - 1, 0)),
            whole(8, width),
            whole(2, 128, 256),
        ],
        out_specs=(whole(24, width + 128), whole(24, width + 128), whole(4, 16, 128)),
        scratch_shapes=[pltpu.VMEM((2, 24, width + 128), F32)],
    )(got_odd, got_even, west, east, swept, swept, traces, jnp.asarray(column_matrices()))
    got_y_even = lax.ppermute(send_y_even, "gy", y_even)
    got_y_odd = lax.ppermute(send_y_odd, "gy", y_odd)
    updated, filtered, outer = call(
        functools.partial(finish_kernel, width, height),
        (full, full, shape((2, 2, 18, 8, 128), F32)),
        (60_000_000, 4_000_000),
        in_specs=[VMEM] * 3 + [HBM] * 2,
        out_specs=(HBM, HBM, VMEM),
        input_output_aliases={3: 0, 4: 1},
        scratch_shapes=[
            pltpu.VMEM((2, 9, height, 128), F32),
            pltpu.VMEM((2, 9, height, 128), F32),
            pltpu.VMEM((2, 9, height, 128), F32),
            DMA((4,)),
        ],
    )(part, swept, fixes, updated, filtered)
    return call(
        functools.partial(row_fix_kernel, width, height),
        (full, full),
        (4_000_000, 1_000_000),
        in_specs=[VMEM] * 7 + [HBM] * 2,
        out_specs=(HBM, HBM),
        input_output_aliases={7: 0, 8: 1},
        scratch_shapes=[pltpu.VMEM((2, 2, 9, 8, width), F32), DMA((4,))],
    )(got_y_even, got_y_odd, send_y_even, send_y_odd, jnp.asarray(row_matrices()), middle, outer, updated, filtered)


def solution(mesh):
    placed = (P(None, "gy", "gx"), P(None, "gy", "gx"), P("gy", "gx"), P("gy", "gx"))
    return jax.shard_map(
        per_device,
        mesh=mesh,
        in_specs=placed,
        out_specs=(P(None, "gy", "gx"), P(None, "gy", "gx")),
        check_vma=False,
    )
```

```python
import functools

import jax
import jax.numpy as jnp
import numpy as np
from jax import lax
from jax.experimental import pallas as pl
from jax.experimental.pallas import tpu as pltpu
from jax.sharding import PartitionSpec as P


HALF = np.arange(3) + 0.5
PARITY = np.array([1.0, -1.0, 1.0])
GAUSS_NODES = (
    -0.932469514203152,
    -0.6612093864662645,
    -0.2386191860831969,
    0.2386191860831969,
    0.6612093864662645,
    0.932469514203152,
)
GAUSS_WEIGHTS = (
    0.1713244923791704,
    0.3607615730481386,
    0.467913934572691,
    0.467913934572691,
    0.3607615730481386,
    0.1713244923791704,
)
HIGHEST = lax.Precision.HIGHEST
F32 = jnp.float32


def legendre_rows(points):
    return np.stack([points * 0.0 + 1.0, points, 1.5 * points * points - 0.5])


def bspline(points):
    magnitude = np.abs(points)
    return np.where(
        magnitude <= 0.5,
        0.75 - magnitude * magnitude,
        np.where(magnitude <= 1.5, 0.5 * (1.5 - magnitude) ** 2, 0.0),
    )


def kernel_value(points):
    return 1.25 * bspline(points) - 0.125 * (bspline(points + 1.0) + bspline(points - 1.0))


def siac_table():
    nodes = np.array(GAUSS_NODES)
    weights = np.array(GAUSS_WEIGHTS)
    kernel_table = np.zeros((5, 3, 3))
    for slot_index in range(5):
        offset = slot_index - 2
        for low_end, high_end in ((-1.0, 0.0), (0.0, 1.0)):
            for node_value, node_weight in zip(GAUSS_NODES, GAUSS_WEIGHTS):
                xi_value = 0.5 * (low_end + high_end) + 0.5 * (high_end - low_end) * node_value
                outer_weight = 0.5 * (high_end - low_end) * node_weight
                breaks = [-1.0, 1.0]
                for spline_knot in (-2.5, -1.5, -0.5, 0.5, 1.5, 2.5):
                    crossing = xi_value - 2.0 * offset - 2.0 * spline_knot
                    if -1.0 < crossing < 1.0:
                        breaks.append(crossing)
                breaks = sorted(breaks)
                for piece_lo, piece_hi in zip(breaks[:-1], breaks[1:]):
                    eta_points = 0.5 * (piece_lo + piece_hi) + 0.5 * (piece_hi - piece_lo) * nodes
                    eta_weights = 0.5 * (piece_hi - piece_lo) * weights
                    samples = (
                        kernel_value(0.5 * xi_value - 0.5 * eta_points - offset) * eta_weights * 0.5
                    )
                    kernel_table[slot_index] += outer_weight * np.outer(
                        legendre_rows(np.array(xi_value)), legendre_rows(eta_points) @ samples
                    )
    table = kernel_table * (np.arange(3)[None, :, None] + 0.5)
    return table.astype(np.float32).astype(np.float64)


TABLE = siac_table()


def tap(k):
    return TABLE[k + 2] if abs(k) <= 2 else np.zeros((3, 3))


def column_matrices():
    out = np.zeros((2, 128, 256))
    for group in range(4):
        base = 32 * group
        for b in range(3):
            for a in range(3):
                m_out = 3 * a + b
                for i in range(3):
                    col = base + 3 * m_out + i
                    for side, (first, near, far) in enumerate(((-2, -1, 0), (3, 2, 3))):
                        for c in range(3):
                            for j in range(2):
                                out[side, base + 2 * (3 * c + b) + j, col] += tap(first + j - i)[a, c]
                        flux = tap(near - i)[a] @ -HALF + tap(far - i)[a] @ (HALF * PARITY)
                        out[side, base + 18 + b, col] += flux
                out[0, base + 18 + b, 128 + base + m_out] += HALF[a] * PARITY[a]
                out[1, base + 18 + b, 128 + base + m_out] += -HALF[a]
    return out.astype(np.float32)


def row_matrices():
    out = np.zeros((2, 144, 64))
    for a in range(3):
        for b in range(3):
            m_out = 3 * a + b
            for i in range(3):
                for side, (first, near, far, row) in enumerate(((-2, -1, 0, i), (3, 2, 3, 5 + i))):
                    for d in range(3):
                        for j in range(2):
                            out[side, 8 * m_out + row, 9 * j + 3 * a + d] += tap(first + j - i)[b, d]
                    weight = tap(near - i)[b] @ -HALF + tap(far - i)[b] @ (HALF * PARITY)
                    for k in range(-2, 3):
                        for c in range(3):
                            out[side, 8 * m_out + row, 24 + 8 * (k + 2) + 2 + c] += tap(k)[a, c] * weight
            out[0, 72 + 8 * m_out, 24 + 16 + 2 + a] = HALF[b] * PARITY[b]
            out[1, 72 + 8 * m_out + 7, 24 + 16 + 2 + a] = -HALF[b]
    return out.astype(np.float32)


def upwind(speed, inner, outer):
    return jnp.maximum(speed, 0.0) * inner + jnp.minimum(speed, 0.0) * outer


def tile_iota(shape, dim):
    return lax.broadcasted_iota(jnp.int32, shape, dim)


def rows_of(r, count=8, first=0):
    return pl.ds(pl.multiple_of(count * r + first, 8), count)


def turned(value, shift, axis):
    shift %= value.shape[axis]
    return pltpu.roll(value, shift, axis) if shift else value


def update_terms(u, begin, speed_x, speed_y, faces_x, jumps_y):
    sixth_x, sixth_y = 0.6 * speed_x, 0.6 * speed_y
    for b in range(3):
        jump, total = faces_x(b)
        for a in range(3):
            m = 3 * a + b
            value = begin(m) * (1.0 / 3.0) + u[m] * (2.0 / 3.0)
            if a == 0:
                value = value - 0.5 * jump
            elif a == 1:
                value = value + (sixth_x * u[b] - 1.5 * total)
            else:
                value = value + (speed_x * u[3 + b] - 2.5 * jump)
            if b == 0:
                value = value - 0.5 * jumps_y(a, 0)
            elif b == 1:
                value = value + (sixth_y * u[3 * a] - 1.5 * jumps_y(a, 1))
            else:
                value = value + (speed_y * u[3 * a + 1] - 2.5 * jumps_y(a, 0))
            yield m, value


def pack_kernel(width, height, start, sect, vel_x, vel_y, west, east, send_odd, send_even, raw, dense, sems):
    copies = []
    for n, (source, at) in enumerate(((sect, pl.ds(0, 9)), (vel_x, 9), (vel_y, 10), (start, pl.ds(11, 9)))):
        for side in range(2):
            cols = pl.ds(side * (width - 128), 128)
            copies.append(pltpu.make_async_copy(source.at[..., cols], raw.at[side, at], sems.at[2 * n + side]))
            copies[-1].start()
    tiles = height // 8
    lane = tile_iota((8, 128), 1)
    sub = tile_iota((8, 128), 0)
    spot = jnp.bitwise_and(lane, 15)

    def gather(m, carry):
        first = acc = None
        for r in range(tiles):
            rows = slice(8 * r, 8 * r + 8)
            moved = turned(jnp.where(lane < 64, raw[0, m, rows, :], raw[1, m, rows, :]), 16 * r, 1)
            if r == 0:
                first = acc = moved
            else:
                acc = jnp.where(lane >= 16 * r - 8, moved, acc)
        acc = jnp.where(lane >= 120, first, acc)
        dense[m] = jnp.where(spot >= 8, pltpu.roll(acc, 16, 1), acc)
        return carry

    for copy in copies[:2]:
        copy.wait()
    lax.fori_loop(0, 9, gather, 0, unroll=3)
    for copy in copies[2:]:
        copy.wait()
    lax.fori_loop(9, 20, gather, 0, unroll=4)

    def below(value):
        value = pltpu.roll(value, 1, 0)
        return jnp.where(sub == 0, pltpu.roll(value, 16, 1), value)

    def above(value):
        value = pltpu.roll(value, 7, 0)
        return jnp.where(sub == 7, pltpu.roll(value, 112, 1), value)

    modes = [dense[m] for m in range(9)]
    speed_x, speed_y = dense[9], dense[10]
    speed = jnp.where((sub == 0) & (lane < 16), 0.0, 0.1 * (speed_y + below(speed_y)))
    high, low = jnp.maximum(speed, 0.0), jnp.minimum(speed, 0.0)
    jumps, side_traces = [], []
    for a in range(3):
        even, odd = modes[3 * a] + modes[3 * a + 2], modes[3 * a + 1]
        north, south = even + odd, even - odd
        face = high * below(north) + low * south
        face_north = above(face)
        jumps.append((face_north - face, face_north + face))
        side_traces.append(jnp.where(lane < 64, south, north))
    side_traces.append(speed_y)
    speed = jnp.where(spot == 0, 0.0, 0.1 * (speed_x + pltpu.roll(speed_x, 1, 1)))
    high, low = jnp.maximum(speed, 0.0), jnp.minimum(speed, 0.0)
    column_traces = []

    def faces_x(b):
        even, odd = modes[b] + modes[6 + b], modes[3 + b]
        face = high * pltpu.roll(even + odd, 1, 1) + low * (even - odd)
        beyond = pltpu.roll(face, 127, 1)
        column_traces.append((even - odd, even + odd))
        return beyond - face, beyond + face

    values = dict(
        update_terms(modes, lambda m: dense[11 + m], speed_x, speed_y, faces_x, lambda a, kind: jumps[a][kind])
    )
    odd_column = lax.rem(lax.axis_index("gx"), 2) == 1
    both = []
    for side in range(2):
        two, one = (0, 0) if side == 0 else (14, 15)
        low_slots = turned(values[0], -two, 1)
        for m in range(1, 8):
            low_slots = jnp.where(spot >= 2 * m, turned(values[m], 2 * m - two, 1), low_slots)
        high_slots = turned(values[8], -two, 1)
        singles = [column_traces[b][side] for b in range(3)] + [speed_x] * 3
        for n, value in enumerate(singles):
            high_slots = jnp.where(spot >= 2 + n, turned(value, 2 + n - one, 1), high_slots)
        for n, value in enumerate(side_traces):
            high_slots = jnp.where(spot >= 8 + 2 * n, turned(value, 8 + 2 * n - two, 1), high_slots)
        half = jnp.bitwise_and(lane, 16) == 0
        both.append((
            jnp.where(half, low_slots, pltpu.roll(high_slots, 16, 1)),
            jnp.where(half, pltpu.roll(low_slots, 112, 1), high_slots),
        ))
    for half in range(2):
        rows = slice(8 * half, 8 * half + 8)
        west[rows, :] = both[0][half]
        east[rows, :] = both[1][half]
        send_odd[rows, :] = jnp.where(odd_column, both[1][half], both[0][half])
        send_even[rows, :] = jnp.where(odd_column, both[0][half], both[1][half])


def sweep_rows(tiles, load, store):
    sub = tile_iota((8, 128), 0)
    cache = {}

    def rolled(d, r, amount):
        if not 0 <= r < tiles:
            return 0.0
        if (d, r, amount) not in cache:
            cache[d, r, amount] = turned(load(d, r), amount, 0)
        return cache[d, r, amount]

    for r in range(tiles):

        def taken(d, k):
            if k == 0:
                return rolled(d, r, 0)
            if k > 0:
                return jnp.where(sub < 8 - k, rolled(d, r, 8 - k), rolled(d, r + 1, 8 - k))
            return jnp.where(sub >= -k, rolled(d, r, -k), rolled(d, r - 1, -k))

        for b, value in enumerate(sweep([0, 1, 2], taken)):
            store(b, r, value)


def early_kernel(width, height, start, sect, vel_x, vel_y, new, part, swept, traces, s, u, vx, vy, south, sems):
    @pl.when(lax.axis_index("gx") == 0)
    def _():
        local_part(width, height, start, sect, vel_x, vel_y, new, part, swept, traces, s, u, vx, vy, south, sems)


def late_kernel(width, height, *refs):
    inputs, made, (part, swept, traces), outs = refs[:4], refs[4:8], refs[8:11], refs[11:14]
    s, u, vx, vy, south, new, out, sems = refs[14:]
    column = lax.axis_index("gx")

    @pl.when(column != 0)
    def _():
        local_part(width, height, *inputs, new, part, swept, traces, s, u, vx, vy, south, sems)

    @pl.when(column == 0)
    def _():
        for source, target in zip(made, (new, part, swept, traces)):
            target[...] = source[...]

    middle_part(width, height, new, swept, *outs, out, sems)


def local_part(width, height, start, sect, vel_x, vel_y, new, part, swept, traces, s, u, vx, vy, south, sems):
    middle = slice(128, width - 128)
    chunk = 16
    shape = (8, width)
    lane = tile_iota(shape, 1)
    sub = tile_iota(shape, 0)
    nothing = jnp.zeros(shape, F32)

    small = [
        pltpu.make_async_copy(vel_y, vy, sems.at[0]),
        pltpu.make_async_copy(vel_x, vx, sems.at[1]),
    ]
    small[0].start()
    copies = []
    for n in range(height // chunk):
        rows = pl.ds(chunk * n, chunk)
        copies.append(pltpu.make_async_copy(sect.at[:, rows, :], u.at[:, rows, :], sems.at[2 + n]))
        copies[n].start()
    small[1].start()
    begin = []
    for n in range(height // chunk):
        rows = pl.ds(chunk * n, chunk)
        begin.append(pltpu.make_async_copy(start.at[:, rows, :], s.at[:, rows, :], sems.at[2 + height // chunk + n]))
        begin[n].start()

    def south_faces(r, carry):
        rows = rows_of(r)
        speeds = vy[rows, :]
        turned_speed = pltpu.roll(speeds, 1, 0)
        speed = 0.1 * (speeds + jnp.where(sub == 0, carry[3], turned_speed))
        speed = jnp.where((sub == 0) & (r == 0), 0.0, speed)
        high, low = jnp.maximum(speed, 0.0), jnp.minimum(speed, 0.0)
        ahead = []
        for a in range(3):
            even, odd = u[3 * a, rows, :] + u[3 * a + 2, rows, :], u[3 * a + 1, rows, :]
            north = pltpu.roll(even + odd, 1, 0)
            south[a, rows, :] = high * jnp.where(sub == 0, carry[a], north) + low * (even - odd)
            ahead.append(north)
        return (*ahead, turned_speed)

    pieces = width // 128
    narrow = tile_iota((8, 128), 1)

    def sweep_columns(fields, store):
        cache = {}

        def rolled(c, j, amount):
            if not 0 <= j < pieces:
                return 0.0
            if (c, j, amount) not in cache:
                cache[c, j, amount] = turned(fields[c][:, 128 * j : 128 * j + 128], amount, 1)
            return cache[c, j, amount]

        for j in range(pieces):

            def taken(c, k):
                if k == 0:
                    return rolled(c, j, 0)
                if k > 0:
                    return jnp.where(narrow < 128 - k, rolled(c, j, 128 - k), rolled(c, j + 1, 128 - k))
                return jnp.where(narrow >= -k, rolled(c, j, -k), rolled(c, j - 1, -k))

            for a, value in enumerate(sweep([0, 1, 2], taken)):
                store(a, slice(128 * j, 128 * j + 128), value)

    def cells(r, carry):
        rows = rows_of(r)
        after = rows_of(r, first=8)
        modes = [u[m, rows, :] for m in range(9)]
        speed_x, speed_y = vx[rows, :], vy[rows, :]
        speed = jnp.where(lane == 0, 0.0, 0.1 * (speed_x + pltpu.roll(speed_x, 1, 1)))
        high, low = jnp.maximum(speed, 0.0), jnp.minimum(speed, 0.0)
        jump_y, sum_y = [], []
        for a in range(3):
            face = south[a, rows, :]
            above = jnp.where(sub == 7, pltpu.roll(south[a, after, :], 7, 0), pltpu.roll(face, 7, 0))
            jump_y.append(above - face)
            sum_y.append(above + face)

        def faces_x(b):
            even, odd = modes[b] + modes[6 + b], modes[3 + b]
            face = high * pltpu.roll(even + odd, 1, 1) + low * (even - odd)
            beyond = pltpu.roll(face, width - 1, 1)
            return beyond - face, beyond + face

        fields = []
        terms = update_terms(
            modes, lambda m: s[m, rows, :], speed_x, speed_y, faces_x, lambda a, kind: (sum_y if kind else jump_y)[a]
        )
        for m, value in terms:
            part[0, m, rows, :] = value[:, :128]
            new[m, rows, :] = value[:, middle]
            part[1, m, rows, :] = value[:, width - 128 :]
            fields.append(value)
            if len(fields) == 3:

                def keep(a, cols, value, b=m % 3):
                    swept[3 * a + b, rows, cols] = value

                sweep_columns(fields, keep)
                fields = []
        return carry

    small[0].wait()
    carry = (nothing,) * 4
    for n in range(height // chunk):
        copies[n].wait()
        carry = lax.fori_loop(n * chunk // 8, (n + 1) * chunk // 8, south_faces, carry)
    for a in range(3):
        south[a, height : height + 8, :] = nothing
        even = u[3 * a, 0:8, :] + u[3 * a + 2, 0:8, :]
        traces[a : a + 1, :] = (even - u[3 * a + 1, 0:8, :])[0:1]
        even = u[3 * a, height - 8 :, :] + u[3 * a + 2, height - 8 :, :]
        traces[4 + a : 5 + a, :] = (even + u[3 * a + 1, height - 8 :, :])[7:8]
    traces[3:4, :] = vy[0:1, :]
    traces[7:8, :] = vy[height - 1 :, :]
    small[1].wait()
    for n in range(height // chunk):
        begin[n].wait()
        lax.fori_loop(n * chunk // 8, (n + 1) * chunk // 8, cells, 0)


def middle_part(width, height, new, swept, updated, filtered, edges, out, sems):
    middle = slice(128, width - 128)
    inner = slice(8, height - 8)
    tiles = height // 8
    new_copy = pltpu.make_async_copy(new.at[:, inner], updated.at[:, inner, middle], sems.at[10])
    new_copy.start()
    for m in range(9):
        edges[0, m] = new[m, 0:8, :]
        edges[1, m] = new[m, height - 8 :, :]

    def out_copy(a):
        modes = pl.ds(3 * a, 3)
        return pltpu.make_async_copy(out.at[modes, inner], filtered.at[modes, inner, middle], sems.at[11 + a])

    def columns(a, carry):
        def column(j, carry):
            source = pl.ds(pl.multiple_of(128 * j + 128, 128), 128)
            target = pl.ds(pl.multiple_of(128 * j, 128), 128)

            def store(b, r, value):
                if r in (0, tiles - 1):
                    edges[0 if r == 0 else 1, 9 + 3 * a + b, :, target] = value
                else:
                    out[3 * a + b, 8 * r : 8 * r + 8, target] = value

            sweep_rows(tiles, lambda d, r: swept[3 * a + d, 8 * r : 8 * r + 8, source], store)
            return carry

        lax.fori_loop(0, width // 128 - 2, column, 0)
        out_copy(a).start()
        return carry

    lax.fori_loop(0, 3, columns, 0)
    new_copy.wait()
    for a in range(3):
        out_copy(a).wait()


def sweep(fields, shifted):
    outs = [None, None, None]

    def add(i, term):
        outs[i] = term if outs[i] is None else outs[i] + term

    for c in range(3):
        for a in range(3):
            if TABLE[2, a, c] != 0.0 and (a + c) % 2 == 0:
                add(a, float(TABLE[2, a, c]) * shifted(fields[c], 0))
        for k in (1, 2):
            ahead, behind = shifted(fields[c], k), shifted(fields[c], -k)
            even, odd = ahead + behind, ahead - behind
            for a in range(3):
                add(a, float(TABLE[2 + k, a, c]) * (even if (a + c) % 2 == 0 else odd))
    return outs


def edge_kernel(width, got_odd, got_even, west, east, low_rows, high_rows, traces, matrices, send_even, send_odd, fixes, buffer):
    odd_column = lax.rem(lax.axis_index("gx"), 2) == 1
    from_west = jnp.where(odd_column, got_even[...], got_odd[...])
    from_east = jnp.where(odd_column, got_odd[...], got_even[...])
    lane16 = tile_iota((16, 128), 1)
    place = jnp.bitwise_and(lane16, 31)
    is_face = (place >= 18) & (place < 21)

    def speed_of(one, two):
        return 0.1 * (pltpu.roll(one, 125, 1) + pltpu.roll(two, 125, 1))

    own_w, own_e = west[...], east[...]
    face_w = upwind(speed_of(from_west, own_w), from_west, own_w)
    face_e = upwind(speed_of(from_east, own_e), own_e, from_east)
    fix_w = jnp.dot(jnp.where(is_face, face_w, from_west), matrices[0], precision=HIGHEST, preferred_element_type=F32)
    fix_e = jnp.dot(jnp.where(is_face, face_e, from_east), matrices[1], precision=HIGHEST, preferred_element_type=F32)
    fixes[0] = fix_w[:, :128]
    fixes[1] = fix_e[:, :128]
    fixes[2] = fix_w[:, 128:]
    fixes[3] = fix_e[:, 128:]

    lane = tile_iota((8, 128), 1)
    buffer[...] = jnp.zeros_like(buffer)
    for side, tile in enumerate((low_rows, high_rows)):
        half, turn = (0, 0) if side == 0 else (1, 32)
        first = 0 if side == 0 else 6
        near_w = fix_w[8 * half : 8 * half + 8, :128]
        near_e = fix_e[8 * half : 8 * half + 8, :128]
        for m in range(9):
            turn_w, turn_e = (turn - 3 * m) % 128, (turn + 125 - 3 * m) % 128
            add_w = jnp.where(lane < 3, pltpu.roll(near_w, turn_w, 1) if turn_w else near_w, 0.0)
            add_e = jnp.where(lane >= 125, pltpu.roll(near_e, turn_e, 1) if turn_e else near_e, 0.0)
            left = tile[m, :, :128] + add_w
            right = tile[m, :, width - 128 :] + add_e
            middle = tile[m, :, 128 : width - 128]
            for j in range(2):
                row = slice(9 * j + m, 9 * j + m + 1)
                at = slice(first + j, first + j + 1)
                buffer[side, row, 0:128] = left[at]
                buffer[side, row, 128 : width - 128] = middle[at]
                buffer[side, row, width - 128 : width] = right[at]
        for a in range(4):
            row = slice(18 + a, 19 + a)
            buffer[side, row, 0:width] = traces[4 * side + a : 4 * side + a + 1, :]
            source = slice(0, 8) if side == 0 else slice(8, 16)
            base = 24 + 2 * a + (0 if side == 0 else 96)
            line = slice(0, 1) if side == 0 else slice(7, 8)
            left = pltpu.roll(from_west[source], (126 - base) % 128, 1)
            right = pltpu.roll(from_east[source], (-base) % 128, 1)
            halo = jnp.where(lane >= 126, left, jnp.where(lane < 2, right, 0.0))
            buffer[side, row, width : width + 128] = halo[line]
    odd_row = lax.rem(lax.axis_index("gy"), 2) == 1
    for j in range(3):
        rows = slice(8 * j, 8 * j + 8)
        low, high = buffer[0, rows, :], buffer[1, rows, :]
        send_even[rows, :] = jnp.where(odd_row, low, high)
        send_odd[rows, :] = jnp.where(odd_row, high, low)


def finish_kernel(width, height, part, swept, fixes, updated_in, filtered_in, updated, filtered, edges, new, out, tall, sems):
    lane = tile_iota((8, 128), 1)
    tiles = height // 8
    inner = slice(8, height - 8)
    columns = (slice(0, 128), slice(width - 128, width))
    copies = []
    for side in range(2):
        target = 127 * side
        near = lane < 3 if side == 0 else lane >= 125
        for r in range(tiles):
            group, half = r // 2, r % 2
            strip = slice(8 * half, 8 * half + 8)
            rows = slice(8 * r, 8 * r + 8)
            for m in range(9):
                fix = jnp.where(lane == target, turned(fixes[2 + side, strip, :], target - 32 * group - m, 1), 0.0)
                value = part[side, m, rows, :] + fix
                if r in (0, tiles - 1):
                    edges[side, 0 if r == 0 else 1, m] = value
                else:
                    new[side, m, rows, :] = value
                fix = turned(fixes[side, strip, :], 125 * side - 32 * group - 3 * m, 1)
                tall[side, m, rows, :] = swept[m, rows, columns[side]] + jnp.where(near, fix, 0.0)
        copies.append(pltpu.make_async_copy(new.at[side, :, inner], updated.at[:, inner, columns[side]], sems.at[side]))
        copies[-1].start()

    for side in range(2):

        def body(a, carry, side=side):
            def store(b, r, value):
                if r in (0, tiles - 1):
                    edges[side, 0 if r == 0 else 1, 9 + 3 * a + b] = value
                else:
                    out[side, 3 * a + b, 8 * r : 8 * r + 8, :] = value

            sweep_rows(tiles, lambda d, r: tall[side, 3 * a + d, 8 * r : 8 * r + 8, :], store)
            return carry

        lax.fori_loop(0, 3, body, 0)
        copies.append(pltpu.make_async_copy(out.at[side, :, inner], filtered.at[:, inner, columns[side]], sems.at[2 + side]))
        copies[-1].start()
    for copy in copies:
        copy.wait()


def row_fix_kernel(width, height, got_even, got_odd, sent_even, sent_odd, matrices, middle, outer, updated_in, filtered_in, updated, filtered, tiles, sems):
    odd_row = lax.rem(lax.axis_index("gy"), 2)
    copies = []
    for side in range(2):
        use_odd = lax.rem(side + odd_row, 2) == 0
        got = jnp.where(use_odd, got_odd[...], got_even[...])
        own = jnp.where(use_odd, sent_odd[16:24, :], sent_even[16:24, :])
        edge = got[16:24]
        speed = 0.1 * (edge[5:6] + own[5:6])
        face = upwind(speed, edge, own) if side == 0 else upwind(speed, own, edge)
        pieces = [got[:, :width]]
        for k in range(-2, 3):
            pieces.append(turned(face, -k, 1)[:, :width])
        fix = jnp.dot(matrices[side], jnp.concatenate(pieces, axis=0), precision=HIGHEST, preferred_element_type=F32)
        for n, first in enumerate((72, 0)):
            for m in range(9):
                add = fix[first + 8 * m : first + 8 * m + 8]
                tiles[side, n, m, :, 0:128] = outer[0, side, 9 * n + m] + add[:, :128]
                tiles[side, n, m, :, 128 : width - 128] = middle[side, 9 * n + m] + add[:, 128 : width - 128]
                tiles[side, n, m, :, width - 128 : width] = outer[1, side, 9 * n + m] + add[:, width - 128 :]
        rows = slice(0, 8) if side == 0 else slice(height - 8, height)
        for n, target in enumerate((updated, filtered)):
            copies.append(pltpu.make_async_copy(tiles.at[side, n], target.at[:, rows], sems.at[2 * side + n]))
            copies[-1].start()
    for copy in copies:
        copy.wait()


def swap_pairs(count, offset):
    pairs = []
    for i in range(offset, count + offset, 2):
        one, two = i % count, (i + 1) % count
        pairs += [(one, two), (two, one)]
    return pairs


VMEM = pl.BlockSpec(memory_space=pltpu.VMEM)
HBM = pl.BlockSpec(memory_space=pltpu.HBM)
DMA = pltpu.SemaphoreType.DMA


def call(kernel, out_shape, work, grant=24 << 20, **options):
    return pl.pallas_call(
        kernel,
        out_shape=out_shape,
        compiler_params=pltpu.CompilerParams(vmem_limit_bytes=grant),
        cost_estimate=pl.CostEstimate(flops=work[0], bytes_accessed=work[1], transcendentals=0),
        **options,
    )


def per_device(start_coeffs, section_coeffs, vel_x, vel_y):
    height, width = vel_x.shape
    shape = jax.ShapeDtypeStruct
    full = shape((9, height, width), F32)
    pack = shape((16, 128), F32)
    inputs = (start_coeffs, section_coeffs, vel_x, vel_y)
    inputs = tuple(pltpu.with_memory_space_constraint(x, pltpu.HBM) for x in inputs)
    west, east, send_odd, send_even = call(
        functools.partial(pack_kernel, width, height),
        (pack,) * 4,
        (20_000_000, 1_400_000),
        in_specs=[HBM] * 4,
        out_specs=(VMEM,) * 4,
        scratch_shapes=[pltpu.VMEM((2, 20, height, 128), F32), pltpu.VMEM((20, 8, 128), F32), DMA((8,))],
    )(*inputs)
    x_odd, x_even = swap_pairs(lax.axis_size("gx"), 1), swap_pairs(lax.axis_size("gx"), 0)
    y_odd, y_even = swap_pairs(lax.axis_size("gy"), 1), swap_pairs(lax.axis_size("gy"), 0)
    got_even = lax.ppermute(send_even, "gx", x_even)
    got_odd = lax.ppermute(send_odd, "gx", x_odd)
    local = (shape((2, 9, height, 128), F32), full, shape((8, width), F32))
    inner = shape((9, height, width - 256), F32)
    room = [
        pltpu.VMEM((9, height, width), F32),
        pltpu.VMEM((9, height, width), F32),
        pltpu.VMEM((height, width), F32),
        pltpu.VMEM((height, width), F32),
        pltpu.VMEM((3, height + 8, width), F32),
    ]
    made = call(
        functools.partial(early_kernel, width, height),
        (inner, *local),
        (100_000_000, 5_000_000),
        in_specs=[HBM] * 4,
        out_specs=(VMEM,) * 4,
        scratch_shapes=[*room, DMA((14,))],
    )(*inputs)
    part, swept, traces, updated, filtered, middle = call(
        functools.partial(late_kernel, width, height),
        (*local, full, full, shape((2, 18, 8, width - 256), F32)),
        (120_000_000, 5_000_000),
        in_specs=[HBM] * 4 + [VMEM] * 4,
        out_specs=(VMEM, VMEM, VMEM, HBM, HBM, VMEM),
        scratch_shapes=[
            *room,
            pltpu.VMEM((9, height, width - 256), F32),
            pltpu.VMEM((9, height, width - 256), F32),
            DMA((14,)),
        ],
    )(*inputs, *made)
    tall = shape((24, width + 128), F32)
    whole = lambda *dims: pl.BlockSpec(dims, lambda i: (0,) * len(dims))
    send_y_even, send_y_odd, fixes = call(
        functools.partial(edge_kernel, width),
        (tall, tall, shape((4, 16, 128), F32)),
        (4_000_000, 1_000_000),
        grid=(1,),
        in_specs=[whole(16, 128)] * 4
        + [
            pl.BlockSpec((9, 8, width), lambda i: (0, 0, 0)),
            pl.BlockSpec((9, 8, width), lambda i: (0, height // 8 - 1, 0)),
            whole(8, width),
            whole(2, 128, 256),
        ],
        out_specs=(whole(24, width + 128), whole(24, width + 128), whole(4, 16, 128)),
        scratch_shapes=[pltpu.VMEM((2, 24, width + 128), F32)],
    )(got_odd, got_even, west, east, swept, swept, traces, jnp.asarray(column_matrices()))
    got_y_even = lax.ppermute(send_y_even, "gy", y_even)
    got_y_odd = lax.ppermute(send_y_odd, "gy", y_odd)
    updated, filtered, outer = call(
        functools.partial(finish_kernel, width, height),
        (full, full, shape((2, 2, 18, 8, 128), F32)),
        (60_000_000, 4_000_000),
        in_specs=[VMEM] * 3 + [HBM] * 2,
        out_specs=(HBM, HBM, VMEM),
        input_output_aliases={3: 0, 4: 1},
        scratch_shapes=[
            pltpu.VMEM((2, 9, height, 128), F32),
            pltpu.VMEM((2, 9, height, 128), F32),
            pltpu.VMEM((2, 9, height, 128), F32),
            DMA((4,)),
        ],
    )(part, swept, fixes, updated, filtered)
    return call(
        functools.partial(row_fix_kernel, width, height),
        (full, full),
        (4_000_000, 1_000_000),
        in_specs=[VMEM] * 7 + [HBM] * 2,
        out_specs=(HBM, HBM),
        input_output_aliases={7: 0, 8: 1},
        scratch_shapes=[pltpu.VMEM((2, 2, 9, 8, width), F32), DMA((4,))],
    )(got_y_even, got_y_odd, send_y_even, send_y_odd, jnp.asarray(row_matrices()), middle, outer, updated, filtered)


def solution(mesh):
    placed = (P(None, "gy", "gx"), P(None, "gy", "gx"), P("gy", "gx"), P("gy", "gx"))
    return jax.shard_map(
        per_device,
        mesh=mesh,
        in_specs=placed,
        out_specs=(P(None, "gy", "gx"), P(None, "gy", "gx")),
        check_vma=False,
    )
```
